128 devices in a mesh: dp: 8 (over z, x_hi), group: 16 (over x_lo, y, core).
Axes of the slice: x: 4 (x_hi: 2, x_lo: 2; x = x_hi * 2 + x_lo), y: 4, z: 4, core: 2. Of those that a mesh axis runs over, the one named last changes fastest.
Arguments:
- images: bfloat16 [128, 8, 8, 4096], P('dp', None, None, 'group'), may hold values from -6 to 6
- cotangent: bfloat16 [128, 8, 8, 4096], P('dp', None, None, 'group'), may hold values from -6 to 6
- conv_weight: bfloat16 [2, 576, 4096], P(None, 'dp', 'group'), may hold values from -0.25 to 0.25
- mix_weight: bfloat16 [2, 4096, 4096], P(None, 'group', 'dp'), may hold values from -0.09375 to 0.09375
Outputs:
- features_out: bfloat16 [128, 8, 8, 4096], P('dp', None, None, 'group')
- grad_images: bfloat16 [128, 8, 8, 4096], P('dp', None, None, 'group')
- grad_conv: float32 [2, 576, 4096], P(None, 'dp', 'group')
- grad_mix: float32 [2, 4096, 4096], P(None, 'group', 'dp')
The draws below stay inside these ranges and needn't reach their ends.
All inputs are finite; a program needn't handle non-finite values.
Results may differ from the reference program's by a relative error of at most 0.022.
Values may be sent and summed in bfloat16 or wider, within the bound.
A program may use at most 192 MiB of HBM per device.

```python
import math
import jax
import jax.numpy as jnp
from jax import lax

GROUPS = 64
GW = 64
SIDE = 8
LAYERS = 2
C = 4096
IMAGES = 128
N_GROUP = 16


def block_scale(own_key, extent, split, smallest, high):
    loudness, own = 1.0, jax.random.fold_in(own_key, 6)
    for dim, parts in split:
        heights = jnp.exp(jax.random.uniform(jax.random.fold_in(own, dim), (parts,), jnp.float32, smallest / len(split), high / len(split)))
        loudness = loudness * jnp.repeat(heights, extent[dim] // parts).reshape([-1 if axis == dim else 1 for axis in range(len(extent))])
    return loudness


def centred(key, shape, spread, most, cuts=(), dtype=jnp.bfloat16):
    entries = jax.random.normal(key, shape, jnp.float32) * spread
    if len(cuts) > 0:
        entries = block_scale(key, shape, cuts, -0.22, 0.18) * entries
    return jnp.clip(entries, min=-most, max=most).astype(dtype)


def setup_inputs(seed: int = 0) -> dict:
    splits = jax.random.split(jax.random.key(seed), 5)
    images = centred(splits[0], (IMAGES, SIDE, SIDE, C), 1.0, 6.0, ((0, 8), (3, 16)))
    cotangent = centred(splits[1], (IMAGES, SIDE, SIDE, C), 1.0, 6.0, ((0, 8), (3, 16)))
    conv_weight = centred(splits[2], (LAYERS, 9 * GW, C), (9 * GW) ** -0.5, 0.25, ((1, 8), (2, 16)))
    mix_weight = centred(splits[3], (LAYERS, C, C), C ** -0.5, 0.09375, ((1, 16), (2, 8)))
    return dict(images=images, cotangent=cotangent, conv_weight=conv_weight, mix_weight=mix_weight)


def make_patches(field):
    side_cells = field.shape[1]
    padded = jnp.pad(field, ((0, 0), (1, 1), (1, 1), (0, 0)))
    tap_list = [padded[:, row_shift:row_shift + side_cells, col_shift:col_shift + side_cells, :] for row_shift in range(3) for col_shift in range(3)]
    return jnp.stack(tap_list, axis=3).reshape(-1, 9, field.shape[3])

def fold_patches(pieces, batch_size, side_cells):
    pieces = pieces.reshape(batch_size, side_cells, side_cells, 9, pieces.shape[2])
    summed = jnp.zeros((batch_size, side_cells + 2, side_cells + 2, pieces.shape[4]), jnp.float32)
    for tap_index in range(9):
        row_shift = tap_index // 3
        col_shift = tap_index % 3
        summed = summed + jnp.pad(pieces[:, :, :, tap_index, :], ((0, 0), (row_shift, 2 - row_shift), (col_shift, 2 - col_shift), (0, 0)))
    return summed[:, 1:side_cells + 1, 1:side_cells + 1, :]

def silu_slope(value):
    sigmoid_v = jax.nn.sigmoid(value)
    return sigmoid_v * (1.0 + value * (1.0 - sigmoid_v))

def block_mix(hidden, weight):
    pixel_count, channels = hidden.shape
    block_width = channels // N_GROUP
    hidden_blocks = hidden.reshape(pixel_count, N_GROUP, block_width).transpose(1, 0, 2)
    weight_blocks = weight.reshape(N_GROUP, block_width, channels)

    def add_block(total, pair):
        term = jnp.dot(pair[0], pair[1], preferred_element_type=jnp.float32)
        rounded = lax.optimization_barrier(term.astype(jnp.bfloat16))
        return (total + rounded.astype(jnp.float32), None)
    total, _ = lax.scan(add_block, jnp.zeros((pixel_count, channels), jnp.float32), (hidden_blocks, weight_blocks))
    return total

def reference(images, cotangent, conv_weight, mix_weight):
    image_count, side_cells, _, channels = images.shape
    pixel_count = image_count * side_cells * side_cells
    grad_scale = 1.0 / math.sqrt(pixel_count)

    def split_groups(field):
        return field.reshape(image_count, side_cells, side_cells, GROUPS, GW).transpose(3, 0, 1, 2, 4)

    def merge_groups(stacked):
        return stacked.transpose(1, 0, 2).reshape(pixel_count, channels)

    def conv_one(pair):
        patches = make_patches(pair[0]).reshape(-1, 9 * GW)
        return jnp.dot(patches, pair[1], preferred_element_type=jnp.float32)
    current = images
    saved = []
    for layer in range(LAYERS):
        tap_weights = conv_weight[layer].reshape(9 * GW, GROUPS, GW).transpose(1, 0, 2)
        pre_act = merge_groups(lax.map(conv_one, (split_groups(current), tap_weights)))
        hidden = jax.nn.silu(pre_act).astype(jnp.bfloat16)
        mixed = block_mix(hidden, mix_weight[layer])
        saved.append((current, pre_act, hidden, tap_weights))
        current = (current.reshape(pixel_count, channels).astype(jnp.float32) + mixed).astype(jnp.bfloat16).reshape(images.shape)
    features_out = current

    def back_one(triple):
        patches = make_patches(triple[0]).reshape(-1, 9 * GW)
        weight_term = jnp.dot(patches.T, triple[1], preferred_element_type=jnp.float32)
        patch_term = jnp.dot(triple[1], triple[2].T, preferred_element_type=jnp.float32).reshape(-1, 9, GW)
        return (weight_term, fold_patches(patch_term, image_count, side_cells))
    gradient = cotangent
    conv_grads = []
    mix_grads = []
    for layer in reversed(range(LAYERS)):
        before, pre_act, hidden, tap_weights = saved[layer]
        flat_grad = gradient.reshape(pixel_count, channels)
        grad_mix = jnp.dot(hidden.T, flat_grad, preferred_element_type=jnp.float32) * grad_scale
        grad_hidden = jnp.dot(flat_grad, mix_weight[layer].T, preferred_element_type=jnp.float32)
        grad_pre = (grad_hidden * silu_slope(pre_act)).astype(jnp.bfloat16)
        grad_groups = grad_pre.reshape(pixel_count, GROUPS, GW).transpose(1, 0, 2)
        weight_terms, field_terms = lax.map(back_one, (split_groups(before), grad_groups, tap_weights))
        conv_grad = weight_terms.transpose(1, 0, 2).reshape(9 * GW, channels) * grad_scale
        field_grad = field_terms.transpose(1, 2, 3, 0, 4).reshape(images.shape)
        gradient = (gradient.astype(jnp.float32) + field_grad).astype(jnp.bfloat16)
        conv_grads.insert(0, conv_grad)
        mix_grads.insert(0, grad_mix)
    return (features_out, gradient, jnp.stack(conv_grads), jnp.stack(mix_grads))
```

```python
import functools
import math

import jax
import jax.numpy as jnp
from jax import lax
from jax.experimental import pallas as pl
from jax.experimental.pallas import tpu as pltpu
from jax.sharding import PartitionSpec as P

GW = 64
CH = 2
F32 = jnp.float32
BF16 = jnp.bfloat16
MESH = pl.DeviceIdType.MESH


def kernel(
    scale, img, cot, cw, mw, feat, gimg, gconv, gmix,
    wbuf, hidg, gg, slope, col, pad, wbd, wbt, cwg, cwf, x1,
    rys, ryr, rxs, rxr, dws, dar, dbs, dbr, dcs_, dcr_, dcf, dcc, dcv,
    cv_s, cv_r, w1_s, w1_r, w2_s, w2_r, w3_s, w3_r, ax_s, ax_r, ay_s, ay_r,
    ry_s, ry_r, rx_s, rx_r, da_s, da_r, db_s, db_r, dc_s, dc_r, de_s, de_r,
):
    d = lax.axis_index("dp")
    g = lax.axis_index("group")
    z, xh = lax.div(d, 2), lax.rem(d, 2)
    c, y, xl = lax.rem(g, 2), lax.rem(lax.div(g, 2), 4), lax.div(g, 8)
    zq, zb = lax.div(z, 2), lax.rem(z, 2)
    zt, xt = 2 * xl + zb, zq
    home = zq == xl
    nrow = img.shape[0]
    rows = nrow // CH
    nimg = rows // 64

    def dev(z_=None, xh_=None, xl_=None, y_=None, c_=None):
        z_ = z if z_ is None else z_
        xh_ = xh if xh_ is None else xh_
        xl_ = xl if xl_ is None else xl_
        y_ = y if y_ is None else y_
        c_ = c if c_ is None else c_
        return {"dp": z_ * 2 + xh_, "group": xl_ * 8 + y_ * 2 + c_}

    def dpdev(o):
        return {"dp": lax.rem(d + o, 8), "group": g}

    def rc(src, dst, ss, rs, to):
        return pltpu.make_async_remote_copy(
            src_ref=src, dst_ref=dst, send_sem=ss, recv_sem=rs, device_id=to, device_id_type=MESH
        )

    def blk(i, n=256):
        return pl.ds(pl.multiple_of(i * n, n), n)

    def rsl(k):
        return pl.ds(k * rows, rows)

    bar = pltpu.get_barrier_semaphore()
    peers = [dev(c_=1 - c), dev(xl_=1 - xl), dev(xl_=1 - xl, c_=1 - c)]
    peers += [dev(y_=lax.rem(y + o, 4)) for o in (1, 2, 3)]
    peers += [dpdev(o) for o in range(1, 8)]
    for p in peers:
        pl.semaphore_signal(bar, inc=1, device_id=p, device_id_type=MESH)

    @pl.when(jnp.logical_not(home))
    def _():
        for h in (0, 1):
            pl.semaphore_signal(bar, inc=1, device_id=dev(z_=zt, xl_=xt, c_=h), device_id_type=MESH)

    pl.semaphore_wait(bar, len(peers) + 2 * lax.rem(zq + xl, 2))

    def w1(l, h):
        src = mw.at[l, :, pl.ds(h * 256, 256)]
        dst = wbuf.at[l, blk(xl * 2 + c), blk(2 * zb + xh)]
        self_ = jnp.logical_and(home, c == h)
        return (
            self_,
            lambda: pltpu.make_async_copy(src, dst, w1_r.at[l, c]),
            lambda: rc(src, dst, w1_s.at[l, h], w1_r.at[l, c], dev(z_=zt, xl_=xt, c_=h)),
        )

    def w1_start(l):
        for h in (0, 1):
            self_, loc, rem = w1(l, h)

            @pl.when(self_)
            def _():
                loc().start()

            @pl.when(jnp.logical_not(self_))
            def _():
                rem().start()

    def piece(l, xh_):
        return wbuf.at[l, blk(zq, 512), blk(2 * zb + xh_)]

    def w1_wait(l):
        for cc in (0, 1):
            part = wbuf.at[l, blk(zq * 2 + cc), blk(2 * zb + xh)]
            rc(part, part, w1_s.at[l, 0], w1_r.at[l, cc], dev(c_=1 - c)).wait_recv()

    def w1_drain(l):
        for h in (0, 1):
            self_, _, rem = w1(l, h)

            @pl.when(jnp.logical_not(self_))
            def _():
                rem().wait_send()

    def w2(l):
        return rc(piece(l, xh), piece(l, xh), w2_s.at[l], w2_r.at[l], dev(xh_=1 - xh))

    def w2_in(l):
        return rc(piece(l, 1 - xh), piece(l, 1 - xh), w2_s.at[l], w2_r.at[l], dev(xh_=1 - xh))

    def w3(l, o, k):
        p = piece(l, xh if k == 0 else 1 - xh)
        return rc(p, p, w3_s.at[l, o - 1, k], w3_r.at[l, o - 1, k], dev(z_=lax.rem(z + o, 4)))

    def w3_in(l, o, k):
        zs = lax.rem(z + 4 - o, 4)
        p = wbuf.at[l, blk(lax.div(zs, 2), 512), blk(2 * lax.rem(zs, 2) + (xh if k == 0 else 1 - xh))]
        return rc(p, p, w3_s.at[l, o - 1, k], w3_r.at[l, o - 1, k], dev(z_=zs))

    def cv(l, o):
        return rc(cw.at[l], cwg.at[l, o], cv_s.at[l, o], cv_r.at[l, o], dpdev(o))

    def w2_start(l):
        w1_wait(l)
        for o in (2, 1, 3):
            w3(l, o, 0).start()
        w2(l).start()

    def w3_start(l):
        w2_in(l).wait_recv()
        for o in (2, 1, 3):
            w3(l, o, 1).start()

    def w_wait(l):
        for o in (1, 2, 3):
            for k in (0, 1):
                w3_in(l, o, k).wait_recv()

    def w_drain(l):
        w1_drain(l)
        w2(l).wait_send()
        for o in (1, 2, 3):
            for k in (0, 1):
                w3(l, o, k).wait_send()

    def conv_weights(l):
        for o in range(1, 8):
            cv(l, o).wait_recv()
        cwf[pl.ds(pl.multiple_of(d * 72, 8), 72), :] = cw[l].astype(F32)
        for o in range(1, 8):
            src = lax.rem(d + 8 - o, 8)
            cwf[pl.ds(pl.multiple_of(src * 72, 8), 72), :] = cwg[l, o].astype(F32)
        ri = lax.div(lax.broadcasted_iota(jnp.int32, (256, 256), 0), GW)
        ci = lax.div(lax.broadcasted_iota(jnp.int32, (256, 256), 1), GW)
        keep = ri == ci
        for t in range(9):
            w = cwf[t * GW : (t + 1) * GW, :]
            full = jnp.where(keep, jnp.concatenate([w] * 4, axis=0), 0.0)
            wbd[l, t * 256 : (t + 1) * 256, :] = full.astype(BF16)
            wbt[l, (8 - t) * 256 : (9 - t) * 256, :] = full.T.astype(BF16)

    def im2col(v):
        v3 = v.reshape(rows // 8, 8, 256)
        j = lax.broadcasted_iota(jnp.int32, v3.shape, 1)
        left = jnp.where(j == 0, 0.0, pltpu.roll(v3, 1, 1))
        right = jnp.where(j == 7, 0.0, pltpu.roll(v3, 7, 1))
        for b, u in enumerate((left, v3, right)):
            pad[b, :, 1:9] = u.reshape(nimg, 8, 8, 256)
        for a in range(3):
            for b in range(3):
                t = 3 * a + b
                col[:, t * 256 : (t + 1) * 256] = pad[b, :, a : a + 8].reshape(rows, 256).astype(BF16)

    def conv_forward(l, k, xf):
        im2col(xf)
        v = jnp.dot(col[...], wbd[l], preferred_element_type=F32)
        s = jax.nn.sigmoid(v)
        slope[l, rsl(k), :] = s * (1.0 + v * (1.0 - s))
        hidg[l, rsl(k), blk(2 * xl + c)] = (v * s).astype(BF16)

    def conv_backward(l, gp):
        im2col(gp)
        return jnp.dot(col[...], wbt[l], preferred_element_type=F32)

    def conv_weight_grad(l, k, xb):
        m = lax.dot_general(xb, col[...], (((0,), (0,)), ((), ())), preferred_element_type=F32)
        ri = lax.div(lax.broadcasted_iota(jnp.int32, (256, 256), 0), GW)
        ci = lax.div(lax.broadcasted_iota(jnp.int32, (256, 256), 1), GW)
        keep = ri == ci
        for t in range(9):
            part = jnp.where(keep, m[:, (8 - t) * 256 : (9 - t) * 256], 0.0)
            part = jnp.sum(part.reshape(4, GW, 256), axis=0)
            if k == 0:
                dcf[l, t * GW : (t + 1) * GW, :] = part
            else:
                dcf[l, t * GW : (t + 1) * GW, :] += part

    def ax(l, k, m):
        s = hidg.at[l, rsl(k), blk(2 * xl + c)]
        xm, cm = m >> 1, m & 1
        to = dev(xl_=(1 - xl) if xm else xl, c_=(1 - c) if cm else c)
        return rc(s, s, ax_s.at[l, k, m - 1], ax_r.at[l, k, m - 1], to)

    def ax_in(l, k, m):
        xm, cm = m >> 1, m & 1
        xs = (1 - xl) if xm else xl
        cs = (1 - c) if cm else c
        s = hidg.at[l, rsl(k), blk(2 * xs + cs)]
        return rc(s, s, ax_s.at[l, k, m - 1], ax_r.at[l, k, m - 1], dev(xl_=xs, c_=cs))

    def ay(l, k, o):
        s = gg.at[l, rsl(k), blk(y)]
        return rc(s, s, ay_s.at[l, k, o - 1], ay_r.at[l, k, o - 1], dev(y_=lax.rem(y + o, 4)))

    def ay_in(l, k, o):
        ys = lax.rem(y + 4 - o, 4)
        s = gg.at[l, rsl(k), blk(ys)]
        return rc(s, s, ay_s.at[l, k, o - 1], ay_r.at[l, k, o - 1], dev(y_=ys))

    def ry(l, k, o):
        yt = lax.rem(y + o, 4)
        return rc(
            rys.at[l, rsl(k), blk(yt)], ryr.at[l, o - 1, rsl(k)],
            ry_s.at[l, k, o - 1], ry_r.at[l, k, o - 1], dev(y_=yt),
        )

    def mix_forward(l, k):
        def body(i, carry):
            o = lax.rem(i + 1, 4)
            yt = lax.rem(y + o, 4)
            p = jnp.dot(hidg[l, rsl(k), :], wbuf[l, :, blk(yt)], preferred_element_type=F32)
            rys[l, rsl(k), blk(yt)] = p.astype(BF16)

            @pl.when(o > 0)
            def _():
                ry(l, k, o).start()

            return carry

        lax.fori_loop(0, 4, body, 0)

    def mixed(l, k):
        for o in (1, 2, 3):
            ry(l, k, o).wait_recv()
        total = rys[l, rsl(k), blk(y)].astype(F32)
        for o in (1, 2, 3):
            total = total + ryr[l, o - 1, rsl(k), :].astype(F32)
        return total

    def rx(l, k, m):
        kb = jnp.bitwise_xor(2 * xl + c, m)
        return rc(
            rxs.at[l, rsl(k), blk(kb)], rxr.at[l, m - 1, rsl(k)],
            rx_s.at[l, k, m - 1], rx_r.at[l, k, m - 1],
            dev(xl_=lax.div(kb, 2), c_=lax.rem(kb, 2)),
        )

    def mix_backward(l, k):
        def body(i, carry):
            m = 3 - i
            kb = jnp.bitwise_xor(2 * xl + c, m)
            p = lax.dot_general(
                gg[l, rsl(k), :], wbuf[l, blk(kb), :], (((1,), (1,)), ((), ())), preferred_element_type=F32
            )
            rxs[l, rsl(k), blk(kb)] = p.astype(BF16)

            @pl.when(m > 0)
            def _():
                rx(l, k, m).start()

            return carry

        lax.fori_loop(0, 4, body, 0)

    def grad_hidden(l, k):
        for m in (1, 2, 3):
            rx(l, k, m).wait_recv()
        total = rxs[l, rsl(k), blk(2 * xl + c)].astype(F32)
        for m in (1, 2, 3):
            total = total + rxr[l, m - 1, rsl(k), :].astype(F32)
        return total

    def da(l, o):
        zo = lax.rem(z + o, 4)
        return rc(
            dws.at[l, blk(lax.div(zo, 2), 512), blk(lax.rem(zo, 2), 512)], dar.at[l, o - 1],
            da_s.at[l, o - 1], da_r.at[l, o - 1], dev(z_=zo),
        )

    def mix_weight_grad(l):
        def body(i, carry):
            o = lax.rem(i + 1, 4)
            zo = lax.rem(z + o, 4)
            rr, cc = blk(lax.div(zo, 2), 512), blk(lax.rem(zo, 2), 512)
            p = lax.dot_general(
                hidg[l, :, rr], gg[l, :, cc], (((0,), (0,)), ((), ())), preferred_element_type=F32
            )
            dws[l, rr, cc] = p.astype(BF16)

            @pl.when(o > 0)
            def _():
                da(l, o).start()

            return carry

        lax.fori_loop(0, 4, body, 0)

    def db(l):
        return rc(dbs.at[l, 1 - xh], dbr.at[l], db_s.at[l], db_r.at[l], dev(xh_=1 - xh))

    def dw_a(l):
        for o in (1, 2, 3):
            da(l, o).wait_recv()
        for h in (0, 1):
            cc = pl.ds(h * 256, 256)
            t = dws[l, blk(zq, 512), blk(2 * zb + h)].astype(F32)
            for o in (1, 2, 3):
                t = t + dar[l, o - 1, :, cc].astype(F32)
            dbs[l, h] = t.astype(BF16)
        db(l).start()

    def dc(l, h):
        src = dcs_.at[l, pl.ds(h * 256, 256)]
        dst = dcr_.at[l, c]
        self_ = jnp.logical_and(home, c == h)
        return (
            self_,
            lambda: pltpu.make_async_copy(src, dst, dc_r.at[l, c]),
            lambda: rc(src, dst, dc_s.at[l, h], dc_r.at[l, c], dev(z_=zt, xl_=xt, c_=h)),
        )

    def dw_b(l):
        db(l).wait_recv()
        t = (dbs[l, xh].astype(F32) + dbr[l].astype(F32)) * scale
        dcs_[l] = t.astype(BF16)
        for h in (0, 1):
            self_, loc, rem = dc(l, h)

            @pl.when(self_)
            def _():
                loc().start()

            @pl.when(jnp.logical_not(self_))
            def _():
                rem().start()

    def dw_c(l):
        for cc in (0, 1):
            part = dcr_.at[l, cc]
            rc(part, part, dc_s.at[l, 0], dc_r.at[l, cc], dev(c_=1 - c)).wait_recv()
            gmix[l, :, cc * 256 : (cc + 1) * 256] = dcr_[l, cc].astype(F32)

    def dw_drain(l):
        for o in (1, 2, 3):
            da(l, o).wait_send()
        db(l).wait_send()
        for h in (0, 1):
            self_, _, rem = dc(l, h)

            @pl.when(jnp.logical_not(self_))
            def _():
                rem().wait_send()

    def de(l, o):
        dt = lax.rem(d + o, 8)
        return rc(dcc.at[l, dt], dcv.at[l, o], de_s.at[l, o], de_r.at[l, o], dpdev(o))

    def conv_grad_send(l):
        for i in range(8):
            dcc[l, i] = dcf[l, i * 72 : (i + 1) * 72, :].astype(BF16)
        for o in range(1, 8):
            de(l, o).start()

    def conv_grad_done(l):
        for o in range(1, 8):
            de(l, o).wait_recv()
        t = dcc[l, d].astype(F32)
        for o in range(1, 8):
            t = t + dcv[l, o].astype(F32)
        gconv[l] = t * scale

    for o in range(1, 8):
        cv(0, o).start()
    w1_start(0)
    gg[1, :, blk(y)] = cot[...]
    for k in range(CH):
        for o in (2, 1, 3):
            ay(1, k, o).start()
    for b in range(3):
        pad[b, :, 0] = jnp.zeros((nimg, 8, 256), F32)
        pad[b, :, 9] = jnp.zeros((nimg, 8, 256), F32)
    w2_start(0)
    conv_weights(0)
    w3_start(0)
    for k in range(CH):
        conv_forward(0, k, img[rsl(k), :].astype(F32))
        for m in (3, 2, 1):
            ax(0, k, m).start()
    for o in range(1, 8):
        cv(1, o).start()
    w1_start(1)
    w2_start(1)
    conv_weights(1)
    w3_start(1)
    w_wait(0)
    for k in range(CH):
        for m in (1, 2, 3):
            ax_in(0, k, m).wait_recv()
        mix_forward(0, k)
    for k in range(CH):
        for o in (1, 2, 3):
            ay_in(1, k, o).wait_recv()
    w_wait(1)
    for k in range(CH):
        mix_backward(1, k)
    for k in range(CH):
        xf = (img[rsl(k), :].astype(F32) + mixed(0, k)).astype(BF16)
        x1[rsl(k), :] = xf
        conv_forward(1, k, xf.astype(F32))
        for m in (3, 2, 1):
            ax(1, k, m).start()
        gp = (grad_hidden(1, k) * slope[1, rsl(k), :]).astype(BF16)
        field = conv_backward(1, gp.astype(F32))
        gg[0, rsl(k), blk(y)] = (cot[rsl(k), :].astype(F32) + field).astype(BF16)
        for o in (2, 1, 3):
            ay(0, k, o).start()
        conv_weight_grad(1, k, x1[rsl(k), :])
    conv_grad_send(1)
    for k in range(CH):
        for m in (1, 2, 3):
            ax_in(1, k, m).wait_recv()
        mix_forward(1, k)
    mix_weight_grad(1)
    for k in range(CH):
        for o in (1, 2, 3):
            ay_in(0, k, o).wait_recv()
        mix_backward(0, k)
    mix_weight_grad(0)
    dw_a(1)
    for k in range(CH):
        gp = (grad_hidden(0, k) * slope[0, rsl(k), :]).astype(BF16)
        field = conv_backward(0, gp.astype(F32))
        gimg[rsl(k), :] = (gg[0, rsl(k), blk(y)].astype(F32) + field).astype(BF16)
        conv_weight_grad(0, k, img[rsl(k), :])
    conv_grad_send(0)
    dw_b(1)
    for k in range(CH):
        feat[rsl(k), :] = (x1[rsl(k), :].astype(F32) + mixed(1, k)).astype(BF16)
    dw_a(0)
    dw_c(1)
    dw_b(0)
    conv_grad_done(1)
    conv_grad_done(0)
    dw_c(0)
    for l in range(2):
        w_drain(l)
        dw_drain(l)
        for o in range(1, 8):
            cv(l, o).wait_send()
            de(l, o).wait_send()
        for k in range(CH):
            for o in (1, 2, 3):
                ay(l, k, o).wait_send()
                ry(l, k, o).wait_send()
                ax(l, k, o).wait_send()
                rx(l, k, o).wait_send()


def per_device(images, cotangent, conv_weight, mix_weight):
    n, s, _, w = images.shape
    nrow = n * s * s
    rows = nrow // CH
    scale = 1.0 / math.sqrt(nrow * lax.axis_size("dp"))
    vm = pl.BlockSpec(memory_space=pltpu.VMEM)
    dma = pltpu.SemaphoreType.DMA
    scratch = [
        pltpu.VMEM((2, 1024, 1024), BF16),
        pltpu.VMEM((2, nrow, 1024), BF16),
        pltpu.VMEM((2, nrow, 1024), BF16),
        pltpu.VMEM((2, nrow, 256), F32),
        pltpu.VMEM((rows, 2304), BF16),
        pltpu.VMEM((3, rows // 64, 10, 8, 256), F32),
        pltpu.VMEM((2, 2304, 256), BF16),
        pltpu.VMEM((2, 2304, 256), BF16),
        pltpu.VMEM((2, 8, 72, 256), BF16),
        pltpu.VMEM((576, 256), F32),
        pltpu.VMEM((nrow, 256), BF16),
        pltpu.VMEM((2, nrow, 1024), BF16),
        pltpu.VMEM((2, 3, nrow, 256), BF16),
        pltpu.VMEM((2, nrow, 1024), BF16),
        pltpu.VMEM((2, 3, nrow, 256), BF16),
        pltpu.VMEM((2, 1024, 1024), BF16),
        pltpu.VMEM((2, 3, 512, 512), BF16),
        pltpu.VMEM((2, 2, 512, 256), BF16),
        pltpu.VMEM((2, 512, 256), BF16),
        pltpu.VMEM((2, 512, 256), BF16),
        pltpu.VMEM((2, 2, 256, 256), BF16),
        pltpu.VMEM((2, 576, 256), F32),
        pltpu.VMEM((2, 8, 72, 256), BF16),
        pltpu.VMEM((2, 8, 72, 256), BF16),
        dma((2, 8)), dma((2, 8)),
        dma((2, 2)), dma((2, 2)),
        dma((2,)), dma((2,)),
        dma((2, 3, 2)), dma((2, 3, 2)),
        dma((2, CH, 3)), dma((2, CH, 3)),
        dma((2, CH, 3)), dma((2, CH, 3)),
        dma((2, CH, 3)), dma((2, CH, 3)),
        dma((2, CH, 3)), dma((2, CH, 3)),
        dma((2, 3)), dma((2, 3)),
        dma((2,)), dma((2,)),
        dma((2, 2)), dma((2, 2)),
        dma((2, 8)), dma((2, 8)),
    ]
    feat, gimg, gconv, gmix = pl.pallas_call(
        functools.partial(kernel, scale),
        name="resblocks",
        out_shape=(
            jax.ShapeDtypeStruct((nrow, w), BF16),
            jax.ShapeDtypeStruct((nrow, w), BF16),
            jax.ShapeDtypeStruct(conv_weight.shape, F32),
            jax.ShapeDtypeStruct(mix_weight.shape, F32),
        ),
        in_specs=[vm] * 4,
        out_specs=[vm] * 4,
        scratch_shapes=scratch,
        compiler_params=pltpu.CompilerParams(
            collective_id=0, has_side_effects=True, vmem_limit_bytes=62 << 20
        ),
    )(images.reshape(nrow, w), cotangent.reshape(nrow, w), conv_weight, mix_weight)
    return feat.reshape(images.shape), gimg.reshape(images.shape), gconv, gmix


def solution(mesh):
    specs = (
        P("dp", None, None, "group"),
        P("dp", None, None, "group"),
        P(None, "dp", "group"),
        P(None, "group", "dp"),
    )
    return jax.shard_map(per_device, mesh=mesh, in_specs=specs, out_specs=specs, check_vma=False)
```

```python
import functools
import math

import jax
import jax.numpy as jnp
from jax import lax
from jax.experimental import pallas as pl
from jax.experimental.pallas import tpu as pltpu
from jax.sharding import PartitionSpec as P

GW = 64
CH = 2
F32 = jnp.float32
BF16 = jnp.bfloat16
MESH = pl.DeviceIdType.MESH


def kernel(
    scale, img, cot, cw, mw, feat, gimg, gconv, gmix,
    wbuf, hidg, gg, slope, col, pad, wbd, wbt, cwg, cwf, x1,
    rys, ryr, rxs, rxr, tmp, quad, dws, dar, dbs, dbr, dcs_, dcr_, dcf, dcc, dcv,
    cv_s, cv_r, w1_s, w1_r, w2_s, w2_r, w3_s, w3_r, ax_s, ax_r, ay_s, ay_r,
    ry_s, ry_r, rx_s, rx_r, da_s, da_r, db_s, db_r, dc_s, dc_r, de_s, de_r,
):
    d = lax.axis_index("dp")
    g = lax.axis_index("group")
    z, xh = lax.div(d, 2), lax.rem(d, 2)
    c, y, xl = lax.rem(g, 2), lax.rem(lax.div(g, 2), 4), lax.div(g, 8)
    zq, zb = lax.div(z, 2), lax.rem(z, 2)
    zt, xt = 2 * xl + zb, zq
    home = zq == xl
    nrow = img.shape[0]
    rows = nrow // CH
    nimg = rows // 64

    def dev(z_=None, xh_=None, xl_=None, y_=None, c_=None):
        z_ = z if z_ is None else z_
        xh_ = xh if xh_ is None else xh_
        xl_ = xl if xl_ is None else xl_
        y_ = y if y_ is None else y_
        c_ = c if c_ is None else c_
        return {"dp": z_ * 2 + xh_, "group": xl_ * 8 + y_ * 2 + c_}

    def dpdev(o):
        return {"dp": lax.rem(d + o, 8), "group": g}

    def rc(src, dst, ss, rs, to):
        return pltpu.make_async_remote_copy(
            src_ref=src, dst_ref=dst, send_sem=ss, recv_sem=rs, device_id=to, device_id_type=MESH
        )

    def blk(i, n=256):
        return pl.ds(pl.multiple_of(i * n, n), n)

    def rsl(k):
        return pl.ds(pl.multiple_of(k * rows, rows), rows)

    bar = pltpu.get_barrier_semaphore()
    peers = [dev(c_=1 - c), dev(xl_=1 - xl), dev(xl_=1 - xl, c_=1 - c)]
    peers += [dev(y_=lax.rem(y + o, 4)) for o in (1, 2, 3)]
    peers += [dpdev(o) for o in range(1, 8)]
    for p in peers:
        pl.semaphore_signal(bar, inc=1, device_id=p, device_id_type=MESH)

    @pl.when(jnp.logical_not(home))
    def _():
        for h in (0, 1):
            pl.semaphore_signal(bar, inc=1, device_id=dev(z_=zt, xl_=xt, c_=h), device_id_type=MESH)

    pl.semaphore_wait(bar, len(peers) + 2 * lax.rem(zq + xl, 2))

    def w1(l, h):
        src = mw.at[l, :, pl.ds(h * 256, 256)]
        dst = wbuf.at[l, blk(xl * 2 + c), blk(2 * zb + xh)]
        self_ = jnp.logical_and(home, c == h)
        return (
            self_,
            lambda: pltpu.make_async_copy(src, dst, w1_r.at[l, c]),
            lambda: rc(src, dst, w1_s.at[l, h], w1_r.at[l, c], dev(z_=zt, xl_=xt, c_=h)),
        )

    def w1_start(l):
        for h in (0, 1):
            self_, loc, rem = w1(l, h)

            @pl.when(self_)
            def _():
                loc().start()

            @pl.when(jnp.logical_not(self_))
            def _():
                rem().start()

    def piece(l, xh_):
        return wbuf.at[l, blk(zq, 512), blk(2 * zb + xh_)]

    def w1_wait(l):
        for cc in (0, 1):
            part = wbuf.at[l, blk(zq * 2 + cc), blk(2 * zb + xh)]
            rc(part, part, w1_s.at[l, 0], w1_r.at[l, cc], dev(c_=1 - c)).wait_recv()

    def w1_drain(l):
        for h in (0, 1):
            self_, _, rem = w1(l, h)

            @pl.when(jnp.logical_not(self_))
            def _():
                rem().wait_send()

    def w2(l):
        return rc(piece(l, xh), piece(l, xh), w2_s.at[l], w2_r.at[l], dev(xh_=1 - xh))

    def w2_in(l):
        return rc(piece(l, 1 - xh), piece(l, 1 - xh), w2_s.at[l], w2_r.at[l], dev(xh_=1 - xh))

    def zto(s):
        return lax.rem(z + 1 + 2 * s, 4)

    def zpiece(l, zs, k):
        return wbuf, lax.div(zs, 2), 2 * lax.rem(zs, 2) + (xh if k == 0 else 1 - xh)

    def zfull(l, zs, k):
        w, r, cc = zpiece(l, zs, k)
        return w.at[l, blk(r, 512), blk(cc)]

    def zhalf(l, zs, k, s):
        w, r, cc = zpiece(l, zs, k)
        return w.at[l, blk(2 * r + s), blk(cc)]

    def w3(l, k, s):
        p = zfull(l, z, k)
        return rc(p, p, w3_s.at[l, k, s], w3_r.at[l, k, s], dev(z_=zto(s)))

    def w3_in(l, k, s):
        p = zfull(l, zto(1 - s), k)
        return rc(p, p, w3_s.at[l, k, s], w3_r.at[l, k, s], dev(z_=zto(s)))

    def w3f(l, k, s):
        p = zhalf(l, zto(1 - s), k, s)
        return rc(p, p, w3_s.at[l, k, 2 + s], w3_r.at[l, k, 2 + s], dev(z_=zto(s)))

    def w3f_in(l, k, s):
        p = zhalf(l, lax.rem(z + 2, 4), k, s)
        return rc(p, p, w3_s.at[l, k, 2 + s], w3_r.at[l, k, 2 + s], dev(z_=zto(s)))

    def cv(l, o):
        return rc(cw.at[l], cwg.at[l, o], cv_s.at[l, o], cv_r.at[l, o], dpdev(o))

    def w2_start(l):
        w1_wait(l)
        w2(l).start()
        for s in (0, 1):
            w3(l, 0, s).start()

    def w3_start(l):
        w2_in(l).wait_recv()
        for s in (0, 1):
            w3(l, 1, s).start()

    def w_forward(l, k):
        for s in (0, 1):
            w3_in(l, k, s).wait_recv()
            w3f(l, k, s).start()

    def w_wait(l):
        for k in (0, 1):
            for s in (0, 1):
                w3f_in(l, k, s).wait_recv()

    def w_drain(l):
        w1_drain(l)
        w2(l).wait_send()
        for k in (0, 1):
            for s in (0, 1):
                w3(l, k, s).wait_send()
                w3f(l, k, s).wait_send()

    def conv_weights(l):
        for o in range(1, 8):
            cv(l, o).wait_recv()
        cwf[pl.ds(pl.multiple_of(d * 72, 8), 72), :] = cw[l].astype(F32)
        for o in range(1, 8):
            src = lax.rem(d + 8 - o, 8)
            cwf[pl.ds(pl.multiple_of(src * 72, 8), 72), :] = cwg[l, o].astype(F32)
        ri = lax.div(lax.broadcasted_iota(jnp.int32, (256, 256), 0), GW)
        ci = lax.div(lax.broadcasted_iota(jnp.int32, (256, 256), 1), GW)
        keep = ri == ci
        for t in range(9):
            w = cwf[t * GW : (t + 1) * GW, :]
            full = jnp.where(keep, jnp.concatenate([w] * 4, axis=0), 0.0)
            wbd[l, t * 256 : (t + 1) * 256, :] = full.astype(BF16)
            wbt[l, (8 - t) * 256 : (9 - t) * 256, :] = full.T.astype(BF16)

    def im2col(k, v):
        v3 = v.reshape(rows // 8, 8, 256)
        j = lax.broadcasted_iota(jnp.int32, v3.shape, 1)
        left = jnp.where(j == 0, 0.0, pltpu.roll(v3, 1, 1))
        right = jnp.where(j == 7, 0.0, pltpu.roll(v3, 7, 1))
        for b, u in enumerate((left, v3, right)):
            pad[b, :, 1:9] = u.reshape(nimg, 8, 8, 256)
        for a in range(3):
            for b in range(3):
                t = 3 * a + b
                col[k, :, t * 256 : (t + 1) * 256] = pad[b, :, a : a + 8].reshape(rows, 256).astype(BF16)

    def conv_forward(l, k, xf):
        im2col(k, xf)
        v = jnp.dot(col[k], wbd[l], preferred_element_type=F32)
        s = jax.nn.sigmoid(v)
        slope[l, rsl(k), :] = s * (1.0 + v * (1.0 - s))
        hidg[l, rsl(k), blk(2 * xl + c)] = (v * s).astype(BF16)

    def conv_backward(l, k, gp):
        im2col(k, gp)
        return jnp.dot(col[k], wbt[l], preferred_element_type=F32)

    def conv_weight_grad(l, k, xb):
        m = lax.dot_general(xb, col[k], (((0,), (0,)), ((), ())), preferred_element_type=F32)
        ri = lax.div(lax.broadcasted_iota(jnp.int32, (256, 256), 0), GW)
        ci = lax.div(lax.broadcasted_iota(jnp.int32, (256, 256), 1), GW)
        keep = ri == ci
        for t in range(9):
            part = jnp.where(keep, m[:, (8 - t) * 256 : (9 - t) * 256], 0.0)
            part = jnp.sum(part.reshape(4, GW, 256), axis=0)
            if k == 0:
                dcf[l, t * GW : (t + 1) * GW, :] = part
            else:
                dcf[l, t * GW : (t + 1) * GW, :] += part

    def ax(l, k, m):
        me = 2 * xl + c
        src = me if m < 3 else jnp.bitwise_xor(me, 2)
        s = hidg.at[l, rsl(k), blk(src)]
        to = dev(xl_=1 - xl) if m == 2 else dev(c_=1 - c)
        return rc(s, s, ax_s.at[l, k, m - 1], ax_r.at[l, k, m - 1], to)

    def ax_in(l, k, m):
        s = hidg.at[l, rsl(k), blk(jnp.bitwise_xor(2 * xl + c, m))]
        return rc(s, s, ax_s.at[l, k, m - 1], ax_r.at[l, k, m - 1], dev(c_=1 - c))

    def ax_start(l, k):
        ax(l, k, 2).start()
        ax(l, k, 1).start()

    def ax_forward(l, k):
        ax_in(l, k, 2).wait_recv()
        ax(l, k, 3).start()

    def ax_wait(l, k):
        for m in (1, 3):
            ax_in(l, k, m).wait_recv()

    def yto(s):
        return lax.rem(y + 1 + 2 * s, 4)

    far = lax.rem(y + 2, 4)
    half = rows // 2

    def hsl(k, s):
        return pl.ds(pl.multiple_of(k * rows + s * half, half), half)

    def ay(l, k, s):
        r = gg.at[l, rsl(k), blk(y)]
        return rc(r, r, ay_s.at[l, k, s], ay_r.at[l, k, s], dev(y_=yto(s)))

    def ay_in(l, k, s):
        r = gg.at[l, rsl(k), blk(yto(1 - s))]
        return rc(r, r, ay_s.at[l, k, s], ay_r.at[l, k, s], dev(y_=yto(s)))

    def ayf(l, k, s):
        r = gg.at[l, hsl(k, s), blk(yto(1 - s))]
        return rc(r, r, ay_s.at[l, k, 2 + s], ay_r.at[l, k, 2 + s], dev(y_=yto(s)))

    def ayf_in(l, k, s):
        r = gg.at[l, hsl(k, s), blk(far)]
        return rc(r, r, ay_s.at[l, k, 2 + s], ay_r.at[l, k, 2 + s], dev(y_=yto(s)))

    def ay_start(l, k):
        for s in (0, 1):
            ay(l, k, s).start()

    def ay_forward(l, k):
        for s in (0, 1):
            ay_in(l, k, s).wait_recv()
            ayf(l, k, s).start()

    def ay_wait(l, k):
        for s in (0, 1):
            ayf_in(l, k, s).wait_recv()

    def ryf(l, k, s):
        return rc(
            rys.at[hsl(k, s), blk(far)], ryr.at[l, 2, hsl(k, s)],
            ry_s.at[l, k, 2 + s], ry_r.at[l, k, 2 + s], dev(y_=yto(s)),
        )

    def ry(l, k, s):
        return rc(
            rys.at[rsl(k), blk(yto(s))], ryr.at[l, s, rsl(k)],
            ry_s.at[l, k, s], ry_r.at[l, k, s], dev(y_=yto(s)),
        )

    def mix_far(l):
        @pl.loop(0, CH)
        def _(k):
            p = jnp.dot(hidg[l, rsl(k), :], wbuf[l, :, blk(far)], preferred_element_type=F32)
            rys[rsl(k), blk(far)] = p.astype(BF16)
            for s in (0, 1):
                ryf(l, k, s).start()

    def mix_near(l):
        @pl.loop(0, 2 * CH)
        def _(i):
            k, s = lax.div(i, 2), lax.rem(i, 2)
            tmp[...] = jnp.dot(hidg[l, rsl(k), :], wbuf[l, :, blk(yto(s))], preferred_element_type=F32)
            ryf(l, k, s).wait_recv()
            tmp[pl.ds(pl.multiple_of(s * half, half), half), :] += ryr[l, 2, hsl(k, s), :].astype(F32)
            rys[rsl(k), blk(yto(s))] = tmp[...].astype(BF16)
            ry(l, k, s).start()

    def mix_own(l):
        @pl.loop(0, CH)
        def _(k):
            p = jnp.dot(hidg[l, rsl(k), :], wbuf[l, :, blk(y)], preferred_element_type=F32)
            rys[rsl(k), blk(y)] = p.astype(BF16)

    def mixed(l, k):
        total = rys[rsl(k), blk(y)].astype(F32)
        for s in (0, 1):
            ry(l, k, s).wait_recv()
            total = total + ryr[l, s, rsl(k), :].astype(F32)
        return total

    def ry_drain(l):
        for k in range(CH):
            for s in (0, 1):
                ry(l, k, s).wait_send()
                ryf(l, k, s).wait_send()

    def rx(l, k, m):
        kb = jnp.bitwise_xor(2 * xl + c, m)
        return rc(
            rxs.at[rsl(k), blk(kb)], rxr.at[l, m - 1, rsl(k)],
            rx_s.at[l, k, m - 1], rx_r.at[l, k, m - 1],
            dev(xl_=1 - xl) if m == 2 else dev(c_=1 - c),
        )

    def back_block(l, k, m):
        kb = jnp.bitwise_xor(2 * xl + c, m)
        return kb, lax.dot_general(
            gg[l, rsl(k), :], wbuf[l, blk(kb), :], (((1,), (1,)), ((), ())), preferred_element_type=F32
        )

    def back_far(l):
        @pl.loop(0, CH)
        def _(k):
            kb, p = back_block(l, k, 3)
            rxs[rsl(k), blk(kb)] = p.astype(BF16)
            rx(l, k, 3).start()

    def back_near(l):
        @pl.loop(0, CH)
        def _(k):
            kb, p = back_block(l, k, 2)
            rx(l, k, 3).wait_recv()
            rxs[rsl(k), blk(kb)] = (p + rxr[l, 2, rsl(k), :].astype(F32)).astype(BF16)
            rx(l, k, 2).start()

    def back_own(l):
        @pl.loop(0, CH)
        def _(k):
            kb, p = back_block(l, k, 1)
            rxs[rsl(k), blk(kb)] = p.astype(BF16)
            rx(l, k, 1).start()
            kb, p = back_block(l, k, 0)
            rxs[rsl(k), blk(kb)] = p.astype(BF16)

    def mix_backward(l):
        back_far(l)
        back_near(l)
        back_own(l)

    def grad_hidden(l, k):
        total = rxs[rsl(k), blk(2 * xl + c)].astype(F32)
        for m in (1, 2):
            rx(l, k, m).wait_recv()
            total = total + rxr[l, m - 1, rsl(k), :].astype(F32)
        return total

    def rx_drain(l):
        for k in range(CH):
            for m in (1, 2, 3):
                rx(l, k, m).wait_send()

    def zrows(zs):
        return blk(lax.div(zs, 2), 512)

    def zcols(zs):
        return blk(lax.rem(zs, 2), 512)

    zfar = lax.rem(z + 2, 4)

    def daf(l, s):
        return rc(
            dws.at[l, blk(2 * lax.div(zfar, 2) + s), zcols(zfar)], dar.at[l, 2, blk(s)],
            da_s.at[l, 2 + s], da_r.at[l, 2 + s], dev(z_=zto(s)),
        )

    def da(l, s):
        zo = zto(s)
        return rc(
            dws.at[l, zrows(zo), zcols(zo)], dar.at[l, s],
            da_s.at[l, s], da_r.at[l, s], dev(z_=zo),
        )

    def weight_quad(l, zo):
        return lax.dot_general(
            hidg[l, :, zrows(zo)], gg[l, :, zcols(zo)], (((0,), (0,)), ((), ())), preferred_element_type=F32
        )

    def mix_weight_grad(l):
        @pl.loop(0, 4)
        def _(i):
            zo = lax.rem(z + jnp.where(i == 0, 2, jnp.where(i == 3, 0, 2 * i - 1)), 4)
            quad[...] = weight_quad(l, zo)

            @pl.when(i == 0)
            def _():
                dws[l, zrows(zo), zcols(zo)] = quad[...].astype(BF16)
                for s in (0, 1):
                    daf(l, s).start()

            for s in (0, 1):

                @pl.when(i == 1 + s)
                def _():
                    daf(l, s).wait_recv()
                    quad[s * 256 : (s + 1) * 256, :] += dar[l, 2, s * 256 : (s + 1) * 256, :].astype(F32)
                    dws[l, zrows(zo), zcols(zo)] = quad[...].astype(BF16)
                    da(l, s).start()

            @pl.when(i == 3)
            def _():
                dws[l, zrows(zo), zcols(zo)] = quad[...].astype(BF16)

    def db(l):
        return rc(dbs.at[l, 1 - xh], dbr.at[l], db_s.at[l], db_r.at[l], dev(xh_=1 - xh))

    def dw_a(l):
        for s in (0, 1):
            da(l, s).wait_recv()
        for h in (0, 1):
            cc = pl.ds(h * 256, 256)
            t = dws[l, blk(zq, 512), blk(2 * zb + h)].astype(F32)
            for s in (0, 1):
                t = t + dar[l, s, :, cc].astype(F32)
            dbs[l, h] = t.astype(BF16)
        db(l).start()

    def dc(l, h):
        src = dcs_.at[l, pl.ds(h * 256, 256)]
        dst = dcr_.at[l, c]
        self_ = jnp.logical_and(home, c == h)
        return (
            self_,
            lambda: pltpu.make_async_copy(src, dst, dc_r.at[l, c]),
            lambda: rc(src, dst, dc_s.at[l, h], dc_r.at[l, c], dev(z_=zt, xl_=xt, c_=h)),
        )

    def dw_b(l):
        db(l).wait_recv()
        t = (dbs[l, xh].astype(F32) + dbr[l].astype(F32)) * scale
        dcs_[l] = t.astype(BF16)
        for h in (0, 1):
            self_, loc, rem = dc(l, h)

            @pl.when(self_)
            def _():
                loc().start()

            @pl.when(jnp.logical_not(self_))
            def _():
                rem().start()

    def dw_c(l):
        for cc in (0, 1):
            part = dcr_.at[l, cc]
            rc(part, part, dc_s.at[l, 0], dc_r.at[l, cc], dev(c_=1 - c)).wait_recv()
            gmix[l, :, cc * 256 : (cc + 1) * 256] = dcr_[l, cc].astype(F32)

    def dw_drain(l):
        for s in (0, 1):
            da(l, s).wait_send()
            daf(l, s).wait_send()
        db(l).wait_send()
        for h in (0, 1):
            self_, _, rem = dc(l, h)

            @pl.when(jnp.logical_not(self_))
            def _():
                rem().wait_send()

    def de(l, o):
        dt = lax.rem(d + o, 8)
        return rc(dcc.at[l, dt], dcv.at[l, o], de_s.at[l, o], de_r.at[l, o], dpdev(o))

    def conv_grad_send(l):
        for i in range(8):
            dcc[l, i] = dcf[l, i * 72 : (i + 1) * 72, :].astype(BF16)
        for o in range(1, 8):
            de(l, o).start()

    def conv_grad_done(l):
        for o in range(1, 8):
            de(l, o).wait_recv()
        t = dcc[l, d].astype(F32)
        for o in range(1, 8):
            t = t + dcv[l, o].astype(F32)
        gconv[l] = t * scale

    for o in range(1, 8):
        cv(0, o).start()
    w1_start(0)
    gg[1, :, blk(y)] = cot[...]
    for k in range(CH):
        ay_start(1, k)
    for b in range(3):
        pad[b, :, 0] = jnp.zeros((nimg, 8, 256), F32)
        pad[b, :, 9] = jnp.zeros((nimg, 8, 256), F32)
    w2_start(0)
    w1_start(1)
    conv_weights(0)
    conv_forward(0, 0, img[rsl(0), :].astype(F32))
    ax_start(0, 0)
    ay_forward(1, 0)
    w3_start(0)
    w_forward(0, 0)
    conv_forward(0, 1, img[rsl(1), :].astype(F32))
    ax_start(0, 1)
    for o in range(1, 8):
        cv(1, o).start()
    ay_forward(1, 1)
    ax_forward(0, 0)
    w_forward(0, 1)
    ax_forward(0, 1)
    conv_weights(1)
    w2_start(1)
    for k in range(CH):
        ax_wait(0, k)
    w_wait(0)
    mix_far(0)
    w3_start(1)
    mix_near(0)
    w_forward(1, 0)
    mix_own(0)
    for k in range(CH):
        ay_wait(1, k)
    w_forward(1, 1)
    w_wait(1)
    mix_backward(1)
    for k in range(CH):
        xf = (img[rsl(k), :].astype(F32) + mixed(0, k)).astype(BF16)
        x1[rsl(k), :] = xf
        conv_forward(1, k, xf.astype(F32))
        ax_start(1, k)
    for k in range(CH):
        gp = (grad_hidden(1, k) * slope[1, rsl(k), :]).astype(BF16)
        field = conv_backward(1, k, gp.astype(F32))
        gg[0, rsl(k), blk(y)] = (cot[rsl(k), :].astype(F32) + field).astype(BF16)
        ay_start(0, k)
        ax_forward(1, k)
    ry_drain(0)
    rx_drain(1)
    for k in range(CH):
        ax_wait(1, k)
    ay_forward(0, 0)
    mix_weight_grad(1)
    ay_forward(0, 1)
    mix_far(1)
    for k in range(CH):
        ay_wait(0, k)
    back_far(0)
    back_near(0)
    mix_weight_grad(0)
    back_own(0)
    mix_near(1)
    mix_own(1)
    dw_a(1)
    for k in range(CH):
        conv_weight_grad(1, k, x1[rsl(k), :])
    conv_grad_send(1)
    dw_b(1)
    for k in range(CH):
        gp = (grad_hidden(0, k) * slope[0, rsl(k), :]).astype(BF16)
        field = conv_backward(0, k, gp.astype(F32))
        gimg[rsl(k), :] = (gg[0, rsl(k), blk(y)].astype(F32) + field).astype(BF16)
        conv_weight_grad(0, k, img[rsl(k), :])
    conv_grad_send(0)
    dw_a(0)
    for k in range(CH):
        feat[rsl(k), :] = (x1[rsl(k), :].astype(F32) + mixed(1, k)).astype(BF16)
    dw_c(1)
    dw_b(0)
    conv_grad_done(1)
    conv_grad_done(0)
    dw_c(0)
    ry_drain(1)
    rx_drain(0)
    for l in range(2):
        w_drain(l)
        dw_drain(l)
        for o in range(1, 8):
            cv(l, o).wait_send()
            de(l, o).wait_send()
        for k in range(CH):
            for m in (1, 2, 3):
                ax(l, k, m).wait_send()
            for s in (0, 1):
                ay(l, k, s).wait_send()
                ayf(l, k, s).wait_send()


def per_device(images, cotangent, conv_weight, mix_weight):
    n, s, _, w = images.shape
    nrow = n * s * s
    rows = nrow // CH
    scale = 1.0 / math.sqrt(nrow * lax.axis_size("dp"))
    vm = pl.BlockSpec(memory_space=pltpu.VMEM)
    dma = pltpu.SemaphoreType.DMA
    scratch = [
        pltpu.VMEM((2, 1024, 1024), BF16),
        pltpu.VMEM((2, nrow, 1024), BF16),
        pltpu.VMEM((2, nrow, 1024), BF16),
        pltpu.VMEM((2, nrow, 256), F32),
        pltpu.VMEM((CH, rows, 2304), BF16),
        pltpu.VMEM((3, rows // 64, 10, 8, 256), F32),
        pltpu.VMEM((2, 2304, 256), BF16),
        pltpu.VMEM((2, 2304, 256), BF16),
        pltpu.VMEM((2, 8, 72, 256), BF16),
        pltpu.VMEM((576, 256), F32),
        pltpu.VMEM((nrow, 256), BF16),
        pltpu.VMEM((nrow, 1024), BF16),
        pltpu.VMEM((2, 3, nrow, 256), BF16),
        pltpu.VMEM((nrow, 1024), BF16),
        pltpu.VMEM((2, 3, nrow, 256), BF16),
        pltpu.VMEM((rows, 256), F32),
        pltpu.VMEM((512, 512), F32),
        pltpu.VMEM((2, 1024, 1024), BF16),
        pltpu.VMEM((2, 3, 512, 512), BF16),
        pltpu.VMEM((2, 2, 512, 256), BF16),
        pltpu.VMEM((2, 512, 256), BF16),
        pltpu.VMEM((2, 512, 256), BF16),
        pltpu.VMEM((2, 2, 256, 256), BF16),
        pltpu.VMEM((2, 576, 256), F32),
        pltpu.VMEM((2, 8, 72, 256), BF16),
        pltpu.VMEM((2, 8, 72, 256), BF16),
        dma((2, 8)), dma((2, 8)),
        dma((2, 2)), dma((2, 2)),
        dma((2,)), dma((2,)),
        dma((2, 2, 4)), dma((2, 2, 4)),
        dma((2, CH, 3)), dma((2, CH, 3)),
        dma((2, CH, 4)), dma((2, CH, 4)),
        dma((2, CH, 4)), dma((2, CH, 4)),
        dma((2, CH, 3)), dma((2, CH, 3)),
        dma((2, 4)), dma((2, 4)),
        dma((2,)), dma((2,)),
        dma((2, 2)), dma((2, 2)),
        dma((2, 8)), dma((2, 8)),
    ]
    feat, gimg, gconv, gmix = pl.pallas_call(
        functools.partial(kernel, scale),
        name="resblocks",
        out_shape=(
            jax.ShapeDtypeStruct((nrow, w), BF16),
            jax.ShapeDtypeStruct((nrow, w), BF16),
            jax.ShapeDtypeStruct(conv_weight.shape, F32),
            jax.ShapeDtypeStruct(mix_weight.shape, F32),
        ),
        in_specs=[vm] * 4,
        out_specs=[vm] * 4,
        scratch_shapes=scratch,
        compiler_params=pltpu.CompilerParams(
            collective_id=0, has_side_effects=True, vmem_limit_bytes=62 << 20
        ),
    )(images.reshape(nrow, w), cotangent.reshape(nrow, w), conv_weight, mix_weight)
    return feat.reshape(images.shape), gimg.reshape(images.shape), gconv, gmix


def solution(mesh):
    specs = (
        P("dp", None, None, "group"),
        P("dp", None, None, "group"),
        P(None, "dp", "group"),
        P(None, "group", "dp"),
    )
    return jax.shard_map(per_device, mesh=mesh, in_specs=specs, out_specs=specs, check_vma=False)
```

```python
import functools
import math

import jax
import jax.numpy as jnp
from jax import lax
from jax.experimental import pallas as pl
from jax.experimental.pallas import tpu as pltpu
from jax.sharding import PartitionSpec as P

GW = 64
CH = 2
F32 = jnp.float32
BF16 = jnp.bfloat16
MESH = pl.DeviceIdType.MESH


def kernel(
    scale, img, cot, cw, mw, feat, gimg, gconv, gmix,
    wbuf, hidg, gg, slope, col, pad, wbd, wbt, cwg, cwf, x1,
    rys, ryr, rxs, rxr, tmp, quad, dws, dar, dbs, dbr, dcs_, dcr_, dcf, dcc, dcv,
    cv_s, cv_r, w1_s, w1_r, w2_s, w2_r, w3_s, w3_r, ax_s, ax_r, ay_s, ay_r,
    ry_s, ry_r, rx_s, rx_r, da_s, da_r, db_s, db_r, dc_s, dc_r, de_s, de_r,
):
    d = lax.axis_index("dp")
    g = lax.axis_index("group")
    z, xh = lax.div(d, 2), lax.rem(d, 2)
    c, y, xl = lax.rem(g, 2), lax.rem(lax.div(g, 2), 4), lax.div(g, 8)
    zq, zb = lax.div(z, 2), lax.rem(z, 2)
    zt, xt = 2 * xl + zb, zq
    home = zq == xl
    nrow = img.shape[0]
    rows = nrow // CH
    nimg = rows // 64

    def dev(z_=None, xh_=None, xl_=None, y_=None, c_=None):
        z_ = z if z_ is None else z_
        xh_ = xh if xh_ is None else xh_
        xl_ = xl if xl_ is None else xl_
        y_ = y if y_ is None else y_
        c_ = c if c_ is None else c_
        return {"dp": z_ * 2 + xh_, "group": xl_ * 8 + y_ * 2 + c_}

    def dpdev(o):
        return {"dp": lax.rem(d + o, 8), "group": g}

    def rc(src, dst, ss, rs, to):
        return pltpu.make_async_remote_copy(
            src_ref=src, dst_ref=dst, send_sem=ss, recv_sem=rs, device_id=to, device_id_type=MESH
        )

    def blk(i, n=256):
        return pl.ds(pl.multiple_of(i * n, n), n)

    def rsl(k):
        return pl.ds(pl.multiple_of(k * rows, rows), rows)

    bar = pltpu.get_barrier_semaphore()
    peers = [dev(c_=1 - c), dev(xl_=1 - xl), dev(xl_=1 - xl, c_=1 - c)]
    peers += [dev(y_=lax.rem(y + o, 4)) for o in (1, 2, 3)]
    peers += [dpdev(o) for o in range(1, 8)]
    for p in peers:
        pl.semaphore_signal(bar, inc=1, device_id=p, device_id_type=MESH)

    @pl.when(jnp.logical_not(home))
    def _():
        for h in (0, 1):
            pl.semaphore_signal(bar, inc=1, device_id=dev(z_=zt, xl_=xt, c_=h), device_id_type=MESH)

    pl.semaphore_wait(bar, len(peers) + 2 * lax.rem(zq + xl, 2))

    def w1(l, h):
        src = mw.at[l, :, pl.ds(h * 256, 256)]
        dst = wbuf.at[l, blk(xl * 2 + c), blk(2 * zb + xh)]
        self_ = jnp.logical_and(home, c == h)
        return (
            self_,
            lambda: pltpu.make_async_copy(src, dst, w1_r.at[l, c]),
            lambda: rc(src, dst, w1_s.at[l, h], w1_r.at[l, c], dev(z_=zt, xl_=xt, c_=h)),
        )

    def w1_start(l):
        for h in (0, 1):
            self_, loc, rem = w1(l, h)

            @pl.when(self_)
            def _():
                loc().start()

            @pl.when(jnp.logical_not(self_))
            def _():
                rem().start()

    def piece(l, xh_):
        return wbuf.at[l, blk(zq, 512), blk(2 * zb + xh_)]

    def w1_wait(l):
        for cc in (0, 1):
            part = wbuf.at[l, blk(zq * 2 + cc), blk(2 * zb + xh)]
            rc(part, part, w1_s.at[l, 0], w1_r.at[l, cc], dev(c_=1 - c)).wait_recv()

    def w1_drain(l):
        for h in (0, 1):
            self_, _, rem = w1(l, h)

            @pl.when(jnp.logical_not(self_))
            def _():
                rem().wait_send()

    def w2(l):
        return rc(piece(l, xh), piece(l, xh), w2_s.at[l], w2_r.at[l], dev(xh_=1 - xh))

    def w2_in(l):
        return rc(piece(l, 1 - xh), piece(l, 1 - xh), w2_s.at[l], w2_r.at[l], dev(xh_=1 - xh))

    def zto(s):
        return lax.rem(z + 1 + 2 * s, 4)

    def zpiece(l, zs, k):
        return wbuf, lax.div(zs, 2), 2 * lax.rem(zs, 2) + (xh if k == 0 else 1 - xh)

    def zfull(l, zs, k):
        w, r, cc = zpiece(l, zs, k)
        return w.at[l, blk(r, 512), blk(cc)]

    def zhalf(l, zs, k, s):
        w, r, cc = zpiece(l, zs, k)
        return w.at[l, blk(2 * r + s), blk(cc)]

    def w3(l, k, s):
        p = zfull(l, z, k)
        return rc(p, p, w3_s.at[l, k, s], w3_r.at[l, k, s], dev(z_=zto(s)))

    def w3_in(l, k, s):
        p = zfull(l, zto(1 - s), k)
        return rc(p, p, w3_s.at[l, k, s], w3_r.at[l, k, s], dev(z_=zto(s)))

    def w3f(l, k, s):
        p = zhalf(l, zto(1 - s), k, s)
        return rc(p, p, w3_s.at[l, k, 2 + s], w3_r.at[l, k, 2 + s], dev(z_=zto(s)))

    def w3f_in(l, k, s):
        p = zhalf(l, lax.rem(z + 2, 4), k, s)
        return rc(p, p, w3_s.at[l, k, 2 + s], w3_r.at[l, k, 2 + s], dev(z_=zto(s)))

    def cv(l, o):
        return rc(cw.at[l], cwg.at[l, o], cv_s.at[l, o], cv_r.at[l, o], dpdev(o))

    def w2_start(l):
        w1_wait(l)
        w2(l).start()
        for s in (0, 1):
            w3(l, 0, s).start()

    def w3_start(l):
        w2_in(l).wait_recv()
        for s in (0, 1):
            w3(l, 1, s).start()

    def w_forward(l, k):
        for s in (0, 1):
            w3_in(l, k, s).wait_recv()
            w3f(l, k, s).start()

    def w_wait(l):
        for k in (0, 1):
            for s in (0, 1):
                w3f_in(l, k, s).wait_recv()

    def w_drain(l):
        w1_drain(l)
        w2(l).wait_send()
        for k in (0, 1):
            for s in (0, 1):
                w3(l, k, s).wait_send()
                w3f(l, k, s).wait_send()

    def conv_weights(l):
        for o in range(1, 8):
            cv(l, o).wait_recv()
        cwf[pl.ds(pl.multiple_of(d * 72, 8), 72), :] = cw[l].astype(F32)
        for o in range(1, 8):
            src = lax.rem(d + 8 - o, 8)
            cwf[pl.ds(pl.multiple_of(src * 72, 8), 72), :] = cwg[l, o].astype(F32)
        ri = lax.div(lax.broadcasted_iota(jnp.int32, (256, 256), 0), GW)
        ci = lax.div(lax.broadcasted_iota(jnp.int32, (256, 256), 1), GW)
        keep = ri == ci
        for t in range(9):
            w = cwf[t * GW : (t + 1) * GW, :]
            full = jnp.where(keep, jnp.concatenate([w] * 4, axis=0), 0.0)
            wbd[l, t * 256 : (t + 1) * 256, :] = full.astype(BF16)
            wbt[l, (8 - t) * 256 : (9 - t) * 256, :] = full.T.astype(BF16)

    def im2col(k, v):
        v3 = v.reshape(rows // 8, 8, 256)
        j = lax.broadcasted_iota(jnp.int32, v3.shape, 1)
        left = jnp.where(j == 0, 0.0, pltpu.roll(v3, 1, 1))
        right = jnp.where(j == 7, 0.0, pltpu.roll(v3, 7, 1))
        for b, u in enumerate((left, v3, right)):
            pad[b, :, 1:9] = u.reshape(nimg, 8, 8, 256)
        for a in range(3):
            for b in range(3):
                t = 3 * a + b
                col[k, :, t * 256 : (t + 1) * 256] = pad[b, :, a : a + 8].reshape(rows, 256).astype(BF16)

    def conv_forward(l, k, xf):
        im2col(k, xf)
        v = jnp.dot(col[k], wbd[l], preferred_element_type=F32)
        s = jax.nn.sigmoid(v)
        slope[l, rsl(k), :] = s * (1.0 + v * (1.0 - s))
        hidg[l, rsl(k), blk(2 * xl + c)] = (v * s).astype(BF16)

    def conv_backward(l, k, gp):
        im2col(k, gp)
        return jnp.dot(col[k], wbt[l], preferred_element_type=F32)

    def conv_weight_grad(l, k, xb):
        m = lax.dot_general(xb, col[k], (((0,), (0,)), ((), ())), preferred_element_type=F32)
        ri = lax.div(lax.broadcasted_iota(jnp.int32, (256, 256), 0), GW)
        ci = lax.div(lax.broadcasted_iota(jnp.int32, (256, 256), 1), GW)
        keep = ri == ci
        for t in range(9):
            part = jnp.where(keep, m[:, (8 - t) * 256 : (9 - t) * 256], 0.0)
            part = jnp.sum(part.reshape(4, GW, 256), axis=0)
            if k == 0:
                dcf[l, t * GW : (t + 1) * GW, :] = part
            else:
                dcf[l, t * GW : (t + 1) * GW, :] += part

    def ax(l, k, m):
        me = 2 * xl + c
        src = me if m < 3 else jnp.bitwise_xor(me, 2)
        s = hidg.at[l, rsl(k), blk(src)]
        to = dev(xl_=1 - xl) if m == 2 else dev(c_=1 - c)
        return rc(s, s, ax_s.at[l, k, m - 1], ax_r.at[l, k, m - 1], to)

    def ax_in(l, k, m):
        s = hidg.at[l, rsl(k), blk(jnp.bitwise_xor(2 * xl + c, m))]
        return rc(s, s, ax_s.at[l, k, m - 1], ax_r.at[l, k, m - 1], dev(c_=1 - c))

    def ax_start(l, k):
        ax(l, k, 2).start()
        ax(l, k, 1).start()

    def ax_forward(l, k):
        ax_in(l, k, 2).wait_recv()
        ax(l, k, 3).start()

    def ax_wait(l, k):
        for m in (1, 3):
            ax_in(l, k, m).wait_recv()

    def yto(s):
        return lax.rem(y + 1 + 2 * s, 4)

    far = lax.rem(y + 2, 4)
    half = rows // 2

    def hsl(k, s):
        return pl.ds(pl.multiple_of(k * rows + s * half, half), half)

    def ay(l, k, s):
        r = gg.at[l, rsl(k), blk(y)]
        return rc(r, r, ay_s.at[l, k, s], ay_r.at[l, k, s], dev(y_=yto(s)))

    def ay_in(l, k, s):
        r = gg.at[l, rsl(k), blk(yto(1 - s))]
        return rc(r, r, ay_s.at[l, k, s], ay_r.at[l, k, s], dev(y_=yto(s)))

    def ayf(l, k, s):
        r = gg.at[l, hsl(k, s), blk(yto(1 - s))]
        return rc(r, r, ay_s.at[l, k, 2 + s], ay_r.at[l, k, 2 + s], dev(y_=yto(s)))

    def ayf_in(l, k, s):
        r = gg.at[l, hsl(k, s), blk(far)]
        return rc(r, r, ay_s.at[l, k, 2 + s], ay_r.at[l, k, 2 + s], dev(y_=yto(s)))

    def ay_start(l, k):
        for s in (0, 1):
            ay(l, k, s).start()

    def ay_forward(l, k):
        for s in (0, 1):
            ay_in(l, k, s).wait_recv()
            ayf(l, k, s).start()

    def ay_wait(l, k):
        for s in (0, 1):
            ayf_in(l, k, s).wait_recv()

    def ryf(l, k, s):
        return rc(
            rys.at[hsl(k, s), blk(far)], ryr.at[l, 2, hsl(k, s)],
            ry_s.at[l, k, 2 + s], ry_r.at[l, k, 2 + s], dev(y_=yto(s)),
        )

    def ry(l, k, s):
        return rc(
            rys.at[rsl(k), blk(yto(s))], ryr.at[l, s, rsl(k)],
            ry_s.at[l, k, s], ry_r.at[l, k, s], dev(y_=yto(s)),
        )

    def mix_far(l):
        @pl.loop(0, CH)
        def _(k):
            p = jnp.dot(hidg[l, rsl(k), :], wbuf[l, :, blk(far)], preferred_element_type=F32)
            rys[rsl(k), blk(far)] = p.astype(BF16)
            for s in (0, 1):
                ryf(l, k, s).start()

    def mix_near(l):
        @pl.loop(0, 2 * CH)
        def _(i):
            k, s = lax.div(i, 2), lax.rem(i, 2)
            tmp[...] = jnp.dot(hidg[l, rsl(k), :], wbuf[l, :, blk(yto(s))], preferred_element_type=F32)
            ryf(l, k, s).wait_recv()
            tmp[pl.ds(pl.multiple_of(s * half, half), half), :] += ryr[l, 2, hsl(k, s), :].astype(F32)
            rys[rsl(k), blk(yto(s))] = tmp[...].astype(BF16)
            ry(l, k, s).start()

    def mix_own(l):
        @pl.loop(0, CH)
        def _(k):
            p = jnp.dot(hidg[l, rsl(k), :], wbuf[l, :, blk(y)], preferred_element_type=F32)
            rys[rsl(k), blk(y)] = p.astype(BF16)

    def mixed(l, k):
        total = rys[rsl(k), blk(y)].astype(F32)
        for s in (0, 1):
            ry(l, k, s).wait_recv()
            total = total + ryr[l, s, rsl(k), :].astype(F32)
        return total

    def ry_drain(l):
        for k in range(CH):
            for s in (0, 1):
                ry(l, k, s).wait_send()
                ryf(l, k, s).wait_send()

    def rx(l, k, m):
        kb = jnp.bitwise_xor(2 * xl + c, m)
        return rc(
            rxs.at[rsl(k), blk(kb)], rxr.at[l, m - 1, rsl(k)],
            rx_s.at[l, k, m - 1], rx_r.at[l, k, m - 1],
            dev(xl_=1 - xl) if m == 2 else dev(c_=1 - c),
        )

    def back_block(l, k, m):
        kb = jnp.bitwise_xor(2 * xl + c, m)
        return kb, lax.dot_general(
            gg[l, rsl(k), :], wbuf[l, blk(kb), :], (((1,), (1,)), ((), ())), preferred_element_type=F32
        )

    def back_far(l):
        @pl.loop(0, CH)
        def _(k):
            kb, p = back_block(l, k, 3)
            rxs[rsl(k), blk(kb)] = p.astype(BF16)
            rx(l, k, 3).start()

    def back_near(l):
        @pl.loop(0, CH)
        def _(k):
            kb, p = back_block(l, k, 2)
            rx(l, k, 3).wait_recv()
            rxs[rsl(k), blk(kb)] = (p + rxr[l, 2, rsl(k), :].astype(F32)).astype(BF16)
            rx(l, k, 2).start()

    def back_own(l):
        @pl.loop(0, CH)
        def _(k):
            kb, p = back_block(l, k, 1)
            rxs[rsl(k), blk(kb)] = p.astype(BF16)
            rx(l, k, 1).start()
            kb, p = back_block(l, k, 0)
            rxs[rsl(k), blk(kb)] = p.astype(BF16)

    def mix_backward(l):
        back_far(l)
        back_near(l)
        back_own(l)

    def grad_hidden(l, k):
        total = rxs[rsl(k), blk(2 * xl + c)].astype(F32)
        for m in (1, 2):
            rx(l, k, m).wait_recv()
            total = total + rxr[l, m - 1, rsl(k), :].astype(F32)
        return total

    def rx_drain(l):
        for k in range(CH):
            for m in (1, 2, 3):
                rx(l, k, m).wait_send()

    def zrows(zs):
        return blk(lax.div(zs, 2), 512)

    def zcols(zs):
        return blk(lax.rem(zs, 2), 512)

    zfar = lax.rem(z + 2, 4)

    def zlanes(zs, h):
        return blk(2 * lax.rem(zs, 2) + jnp.where(h == 0, 1 - xh, xh))

    def daf(l, h, s):
        return rc(
            dws.at[l, blk(2 * lax.div(zfar, 2) + s), zlanes(zfar, h)], dar.at[l, 2, h, blk(s)],
            da_s.at[l, h, 2 + s], da_r.at[l, h, 2 + s], dev(z_=zto(s)),
        )

    def da(l, h, s):
        zo = zto(s)
        return rc(
            dws.at[l, zrows(zo), zlanes(zo, h)], dar.at[l, s, h],
            da_s.at[l, h, s], da_r.at[l, h, s], dev(z_=zo),
        )

    def weight_block(l, zo, h):
        return lax.dot_general(
            hidg[l, :, zrows(zo)], gg[l, :, zlanes(zo, h)], (((0,), (0,)), ((), ())), preferred_element_type=F32
        )

    def weight_far(l):
        @pl.loop(0, 2)
        def _(h):
            dws[l, zrows(zfar), zlanes(zfar, h)] = weight_block(l, zfar, h).astype(BF16)
            for s in (0, 1):
                daf(l, h, s).start()

    def weight_near(l):
        @pl.loop(0, 4)
        def _(i):
            h, s = lax.div(i, 2), lax.rem(i, 2)
            zo = zto(s)
            quad[...] = weight_block(l, zo, h)
            daf(l, h, s).wait_recv()
            hs = blk(s)
            quad[hs, :] += dar[l, 2, h, hs, :].astype(F32)
            dws[l, zrows(zo), zlanes(zo, h)] = quad[...].astype(BF16)
            da(l, h, s).start()

    def weight_own(l):
        @pl.loop(0, 2)
        def _(h):
            dws[l, zrows(z), zlanes(z, h)] = weight_block(l, z, h).astype(BF16)

    def db(l):
        return rc(dbs.at[l, 0], dbr.at[l], db_s.at[l], db_r.at[l], dev(xh_=1 - xh))

    def dw_sum(l, h):
        t = dws[l, zrows(z), zlanes(z, h)].astype(F32)
        for s in (0, 1):
            da(l, h, s).wait_recv()
            t = t + dar[l, s, h].astype(F32)
        dbs[l, h] = t.astype(BF16)
        if h == 0:
            db(l).start()

    def dc(l, h):
        src = dcs_.at[l, pl.ds(h * 256, 256)]
        dst = dcr_.at[l, c]
        self_ = jnp.logical_and(home, c == h)
        return (
            self_,
            lambda: pltpu.make_async_copy(src, dst, dc_r.at[l, c]),
            lambda: rc(src, dst, dc_s.at[l, h], dc_r.at[l, c], dev(z_=zt, xl_=xt, c_=h)),
        )

    def dw_b(l):
        db(l).wait_recv()
        t = (dbs[l, 1].astype(F32) + dbr[l].astype(F32)) * scale
        dcs_[l] = t.astype(BF16)
        for h in (0, 1):
            self_, loc, rem = dc(l, h)

            @pl.when(self_)
            def _():
                loc().start()

            @pl.when(jnp.logical_not(self_))
            def _():
                rem().start()

    def dw_c(l):
        for cc in (0, 1):
            part = dcr_.at[l, cc]
            rc(part, part, dc_s.at[l, 0], dc_r.at[l, cc], dev(c_=1 - c)).wait_recv()
            gmix[l, :, cc * 256 : (cc + 1) * 256] = dcr_[l, cc].astype(F32)

    def dw_drain(l):
        for h in (0, 1):
            for s in (0, 1):
                da(l, h, s).wait_send()
                daf(l, h, s).wait_send()
        db(l).wait_send()
        for h in (0, 1):
            self_, _, rem = dc(l, h)

            @pl.when(jnp.logical_not(self_))
            def _():
                rem().wait_send()

    def de(l, o):
        dt = lax.rem(d + o, 8)
        return rc(dcc.at[l, dt], dcv.at[l, o], de_s.at[l, o], de_r.at[l, o], dpdev(o))

    def conv_grad_send(l):
        for i in range(8):
            dcc[l, i] = dcf[l, i * 72 : (i + 1) * 72, :].astype(BF16)
        for o in range(1, 8):
            de(l, o).start()

    def conv_grad_done(l):
        for o in range(1, 8):
            de(l, o).wait_recv()
        t = dcc[l, d].astype(F32)
        for o in range(1, 8):
            t = t + dcv[l, o].astype(F32)
        gconv[l] = t * scale

    for o in range(1, 8):
        cv(0, o).start()
    w1_start(0)
    gg[1, :, blk(y)] = cot[...]
    for k in range(CH):
        ay_start(1, k)
    for b in range(3):
        pad[b, :, 0] = jnp.zeros((nimg, 8, 256), F32)
        pad[b, :, 9] = jnp.zeros((nimg, 8, 256), F32)
    conv_weights(0)
    w2_start(0)
    conv_forward(0, 0, img[rsl(0), :].astype(F32))
    ax_start(0, 0)
    w3_start(0)
    w1_start(1)
    w_forward(0, 0)
    conv_forward(0, 1, img[rsl(1), :].astype(F32))
    ax_start(0, 1)
    ay_forward(1, 0)
    ax_forward(0, 0)
    w_forward(0, 1)
    w2_start(1)
    for o in range(1, 8):
        cv(1, o).start()
    ay_forward(1, 1)
    ax_forward(0, 1)
    for k in range(CH):
        ax_wait(0, k)
    w_wait(0)
    mix_far(0)
    w3_start(1)
    w_forward(1, 0)
    mix_near(0)
    w_forward(1, 1)
    mix_own(0)
    conv_weights(1)
    for k in range(CH):
        ay_wait(1, k)
    w_wait(1)
    mix_backward(1)
    for k in range(CH):
        xf = (img[rsl(k), :].astype(F32) + mixed(0, k)).astype(BF16)
        x1[rsl(k), :] = xf
        conv_forward(1, k, xf.astype(F32))
        ax_start(1, k)
        gp = (grad_hidden(1, k) * slope[1, rsl(k), :]).astype(BF16)
        field = conv_backward(1, k, gp.astype(F32))
        gg[0, rsl(k), blk(y)] = (cot[rsl(k), :].astype(F32) + field).astype(BF16)
        ay_start(0, k)
    for k in range(CH):
        ax_forward(1, k)
    ay_forward(0, 0)
    ry_drain(0)
    rx_drain(1)
    for k in range(CH):
        ax_wait(1, k)
    weight_far(1)
    ay_forward(0, 1)
    weight_near(1)
    mix_far(1)
    weight_own(1)
    for k in range(CH):
        ay_wait(0, k)
    back_far(0)
    weight_far(0)
    back_near(0)
    back_own(0)
    dw_sum(1, 0)
    weight_near(0)
    dw_sum(1, 1)
    mix_near(1)
    dw_b(1)
    weight_own(0)
    mix_own(1)
    for k in range(CH):
        conv_weight_grad(1, k, x1[rsl(k), :])
    conv_grad_send(1)
    dw_sum(0, 0)
    gp = (grad_hidden(0, 0) * slope[0, rsl(0), :]).astype(BF16)
    field = conv_backward(0, 0, gp.astype(F32))
    gimg[rsl(0), :] = (gg[0, rsl(0), blk(y)].astype(F32) + field).astype(BF16)
    dw_sum(0, 1)
    gp = (grad_hidden(0, 1) * slope[0, rsl(1), :]).astype(BF16)
    field = conv_backward(0, 1, gp.astype(F32))
    gimg[rsl(1), :] = (gg[0, rsl(1), blk(y)].astype(F32) + field).astype(BF16)
    dw_b(0)
    for k in range(CH):
        conv_weight_grad(0, k, img[rsl(k), :])
    conv_grad_send(0)
    for k in range(CH):
        feat[rsl(k), :] = (x1[rsl(k), :].astype(F32) + mixed(1, k)).astype(BF16)
    conv_grad_done(1)
    dw_c(1)
    dw_c(0)
    conv_grad_done(0)
    ry_drain(1)
    rx_drain(0)
    for l in range(2):
        w_drain(l)
        dw_drain(l)
        for o in range(1, 8):
            cv(l, o).wait_send()
            de(l, o).wait_send()
        for k in range(CH):
            for m in (1, 2, 3):
                ax(l, k, m).wait_send()
            for s in (0, 1):
                ay(l, k, s).wait_send()
                ayf(l, k, s).wait_send()


def per_device(images, cotangent, conv_weight, mix_weight):
    n, s, _, w = images.shape
    nrow = n * s * s
    rows = nrow // CH
    scale = 1.0 / math.sqrt(nrow * lax.axis_size("dp"))
    vm = pl.BlockSpec(memory_space=pltpu.VMEM)
    dma = pltpu.SemaphoreType.DMA
    scratch = [
        pltpu.VMEM((2, 1024, 1024), BF16),
        pltpu.VMEM((2, nrow, 1024), BF16),
        pltpu.VMEM((2, nrow, 1024), BF16),
        pltpu.VMEM((2, nrow, 256), F32),
        pltpu.VMEM((CH, rows, 2304), BF16),
        pltpu.VMEM((3, rows // 64, 10, 8, 256), F32),
        pltpu.VMEM((2, 2304, 256), BF16),
        pltpu.VMEM((2, 2304, 256), BF16),
        pltpu.VMEM((2, 8, 72, 256), BF16),
        pltpu.VMEM((576, 256), F32),
        pltpu.VMEM((nrow, 256), BF16),
        pltpu.VMEM((nrow, 1024), BF16),
        pltpu.VMEM((2, 3, nrow, 256), BF16),
        pltpu.VMEM((nrow, 1024), BF16),
        pltpu.VMEM((2, 3, nrow, 256), BF16),
        pltpu.VMEM((rows, 256), F32),
        pltpu.VMEM((512, 256), F32),
        pltpu.VMEM((2, 1024, 1024), BF16),
        pltpu.VMEM((2, 3, 2, 512, 256), BF16),
        pltpu.VMEM((2, 2, 512, 256), BF16),
        pltpu.VMEM((2, 512, 256), BF16),
        pltpu.VMEM((2, 512, 256), BF16),
        pltpu.VMEM((2, 2, 256, 256), BF16),
        pltpu.VMEM((2, 576, 256), F32),
        pltpu.VMEM((2, 8, 72, 256), BF16),
        pltpu.VMEM((2, 8, 72, 256), BF16),
        dma((2, 8)), dma((2, 8)),
        dma((2, 2)), dma((2, 2)),
        dma((2,)), dma((2,)),
        dma((2, 2, 4)), dma((2, 2, 4)),
        dma((2, CH, 3)), dma((2, CH, 3)),
        dma((2, CH, 4)), dma((2, CH, 4)),
        dma((2, CH, 4)), dma((2, CH, 4)),
        dma((2, CH, 3)), dma((2, CH, 3)),
        dma((2, 2, 4)), dma((2, 2, 4)),
        dma((2,)), dma((2,)),
        dma((2, 2)), dma((2, 2)),
        dma((2, 8)), dma((2, 8)),
    ]
    feat, gimg, gconv, gmix = pl.pallas_call(
        functools.partial(kernel, scale),
        name="resblocks",
        out_shape=(
            jax.ShapeDtypeStruct((nrow, w), BF16),
            jax.ShapeDtypeStruct((nrow, w), BF16),
            jax.ShapeDtypeStruct(conv_weight.shape, F32),
            jax.ShapeDtypeStruct(mix_weight.shape, F32),
        ),
        in_specs=[vm] * 4,
        out_specs=[vm] * 4,
        scratch_shapes=scratch,
        compiler_params=pltpu.CompilerParams(
            collective_id=0, has_side_effects=True, vmem_limit_bytes=62 << 20
        ),
    )(images.reshape(nrow, w), cotangent.reshape(nrow, w), conv_weight, mix_weight)
    return feat.reshape(images.shape), gimg.reshape(images.shape), gconv, gmix


def solution(mesh):
    specs = (
        P("dp", None, None, "group"),
        P("dp", None, None, "group"),
        P(None, "dp", "group"),
        P(None, "group", "dp"),
    )
    return jax.shard_map(per_device, mesh=mesh, in_specs=specs, out_specs=specs, check_vma=False)
```

```python
import functools
import math

import jax
import jax.numpy as jnp
from jax import lax
from jax.experimental import pallas as pl
from jax.experimental.pallas import tpu as pltpu
from jax.sharding import PartitionSpec as P

GW = 64
CH = 2
F32 = jnp.float32
BF16 = jnp.bfloat16
MESH = pl.DeviceIdType.MESH


def kernel(
    scale, img, cot, cw, mw, feat, gimg, gconv, gmix,
    wbuf, hidg, gg, slope, col, pad, wbd, wbt, cwg, cwf, x1,
    rys, ryr, rxs, rxr, tmp, quad, dws, dar, dbs, dbr, dcs_, dcr_, dcf, dcc, dcv,
    cv_s, cv_r, w1_s, w1_r, w2_s, w2_r, w3_s, w3_r, ax_s, ax_r, ay_s, ay_r,
    ry_s, ry_r, rx_s, rx_r, da_s, da_r, db_s, db_r, dc_s, dc_r, de_s, de_r,
):
    d = lax.axis_index("dp")
    g = lax.axis_index("group")
    z, xh = lax.div(d, 2), lax.rem(d, 2)
    c, y, xl = lax.rem(g, 2), lax.rem(lax.div(g, 2), 4), lax.div(g, 8)
    zq, zb = lax.div(z, 2), lax.rem(z, 2)
    zt, xt = 2 * xl + zb, zq
    home = zq == xl
    nrow = img.shape[0]
    rows = nrow // CH
    nimg = rows // 64

    def dev(z_=None, xh_=None, xl_=None, y_=None, c_=None):
        z_ = z if z_ is None else z_
        xh_ = xh if xh_ is None else xh_
        xl_ = xl if xl_ is None else xl_
        y_ = y if y_ is None else y_
        c_ = c if c_ is None else c_
        return {"dp": z_ * 2 + xh_, "group": xl_ * 8 + y_ * 2 + c_}

    def dpdev(o):
        return {"dp": lax.rem(d + o, 8), "group": g}

    def rc(src, dst, ss, rs, to):
        return pltpu.make_async_remote_copy(
            src_ref=src, dst_ref=dst, send_sem=ss, recv_sem=rs, device_id=to, device_id_type=MESH
        )

    def blk(i, n=256):
        return pl.ds(pl.multiple_of(i * n, n), n)

    def rsl(k):
        return pl.ds(pl.multiple_of(k * rows, rows), rows)

    bar = pltpu.get_barrier_semaphore()
    peers = [dev(c_=1 - c), dev(xl_=1 - xl), dev(xl_=1 - xl, c_=1 - c)]
    peers += [dev(y_=lax.rem(y + o, 4)) for o in (1, 2, 3)]
    peers += [dpdev(o) for o in range(1, 8)]
    for p in peers:
        pl.semaphore_signal(bar, inc=1, device_id=p, device_id_type=MESH)

    @pl.when(jnp.logical_not(home))
    def _():
        for h in (0, 1):
            pl.semaphore_signal(bar, inc=1, device_id=dev(z_=zt, xl_=xt, c_=h), device_id_type=MESH)

    pl.semaphore_wait(bar, len(peers) + 2 * lax.rem(zq + xl, 2))

    def w1(l, h):
        src = mw.at[l, :, pl.ds(h * 256, 256)]
        dst = wbuf.at[l, blk(xl * 2 + c), blk(2 * zb + xh)]
        self_ = jnp.logical_and(home, c == h)
        return (
            self_,
            lambda: pltpu.make_async_copy(src, dst, w1_r.at[l, c]),
            lambda: rc(src, dst, w1_s.at[l, h], w1_r.at[l, c], dev(z_=zt, xl_=xt, c_=h)),
        )

    def w1_start(l):
        for h in (0, 1):
            self_, loc, rem = w1(l, h)

            @pl.when(self_)
            def _():
                loc().start()

            @pl.when(jnp.logical_not(self_))
            def _():
                rem().start()

    def piece(l, xh_):
        return wbuf.at[l, blk(zq, 512), blk(2 * zb + xh_)]

    def w1_wait(l):
        for cc in (0, 1):
            part = wbuf.at[l, blk(zq * 2 + cc), blk(2 * zb + xh)]
            rc(part, part, w1_s.at[l, 0], w1_r.at[l, cc], dev(c_=1 - c)).wait_recv()

    def w1_drain(l):
        for h in (0, 1):
            self_, _, rem = w1(l, h)

            @pl.when(jnp.logical_not(self_))
            def _():
                rem().wait_send()

    def w2(l):
        return rc(piece(l, xh), piece(l, xh), w2_s.at[l], w2_r.at[l], dev(xh_=1 - xh))

    def w2_in(l):
        return rc(piece(l, 1 - xh), piece(l, 1 - xh), w2_s.at[l], w2_r.at[l], dev(xh_=1 - xh))

    def zto(s):
        return lax.rem(z + 1 + 2 * s, 4)

    def zpiece(l, zs, k):
        return wbuf, lax.div(zs, 2), 2 * lax.rem(zs, 2) + (xh if k == 0 else 1 - xh)

    def zfull(l, zs, k):
        w, r, cc = zpiece(l, zs, k)
        return w.at[l, blk(r, 512), blk(cc)]

    def zhalf(l, zs, k, s):
        w, r, cc = zpiece(l, zs, k)
        return w.at[l, blk(2 * r + s), blk(cc)]

    def w3(l, k, s):
        p = zfull(l, z, k)
        return rc(p, p, w3_s.at[l, k, s], w3_r.at[l, k, s], dev(z_=zto(s)))

    def w3_in(l, k, s):
        p = zfull(l, zto(1 - s), k)
        return rc(p, p, w3_s.at[l, k, s], w3_r.at[l, k, s], dev(z_=zto(s)))

    def w3f(l, k, s):
        p = zhalf(l, zto(1 - s), k, s)
        return rc(p, p, w3_s.at[l, k, 2 + s], w3_r.at[l, k, 2 + s], dev(z_=zto(s)))

    def w3f_in(l, k, s):
        p = zhalf(l, lax.rem(z + 2, 4), k, s)
        return rc(p, p, w3_s.at[l, k, 2 + s], w3_r.at[l, k, 2 + s], dev(z_=zto(s)))

    def cv(l, o):
        return rc(cw.at[l], cwg.at[l, o], cv_s.at[l, o], cv_r.at[l, o], dpdev(o))

    def w2_start(l):
        w1_wait(l)
        w2(l).start()
        for s in (0, 1):
            w3(l, 0, s).start()

    def w3_start(l):
        w2_in(l).wait_recv()
        for s in (0, 1):
            w3(l, 1, s).start()

    def w_forward(l, k):
        for s in (0, 1):
            w3_in(l, k, s).wait_recv()
            w3f(l, k, s).start()

    def w_wait(l):
        for k in (0, 1):
            for s in (0, 1):
                w3f_in(l, k, s).wait_recv()

    def w_drain(l):
        w1_drain(l)
        w2(l).wait_send()
        for k in (0, 1):
            for s in (0, 1):
                w3(l, k, s).wait_send()
                w3f(l, k, s).wait_send()

    def conv_weights(l):
        for o in range(1, 8):
            cv(l, o).wait_recv()
        cwf[pl.ds(pl.multiple_of(d * 72, 8), 72), :] = cw[l].astype(F32)
        for o in range(1, 8):
            src = lax.rem(d + 8 - o, 8)
            cwf[pl.ds(pl.multiple_of(src * 72, 8), 72), :] = cwg[l, o].astype(F32)
        ri = lax.div(lax.broadcasted_iota(jnp.int32, (256, 256), 0), GW)
        ci = lax.div(lax.broadcasted_iota(jnp.int32, (256, 256), 1), GW)
        keep = ri == ci
        for t in range(9):
            w = cwf[t * GW : (t + 1) * GW, :]
            full = jnp.where(keep, jnp.concatenate([w] * 4, axis=0), 0.0)
            wbd[l, t * 256 : (t + 1) * 256, :] = full.astype(BF16)
            wbt[l, (8 - t) * 256 : (9 - t) * 256, :] = full.T.astype(BF16)

    def im2col(k, v):
        v3 = v.reshape(rows // 8, 8, 256)
        j = lax.broadcasted_iota(jnp.int32, v3.shape, 1)
        left = jnp.where(j == 0, 0.0, pltpu.roll(v3, 1, 1))
        right = jnp.where(j == 7, 0.0, pltpu.roll(v3, 7, 1))
        for b, u in enumerate((left, v3, right)):
            pad[b, :, 1:9] = u.reshape(nimg, 8, 8, 256)
        for a in range(3):
            for b in range(3):
                t = 3 * a + b
                col[k, :, t * 256 : (t + 1) * 256] = pad[b, :, a : a + 8].reshape(rows, 256).astype(BF16)

    def conv_forward(l, k, xf):
        im2col(k, xf)
        v = jnp.dot(col[k], wbd[l], preferred_element_type=F32)
        s = jax.nn.sigmoid(v)
        slope[l, rsl(k), :] = s * (1.0 + v * (1.0 - s))
        hidg[l, rsl(k), blk(2 * xl + c)] = (v * s).astype(BF16)

    def conv_backward(l, k, gp):
        im2col(k, gp)
        return jnp.dot(col[k], wbt[l], preferred_element_type=F32)

    def conv_weight_grad(l, k, xb):
        m = lax.dot_general(xb, col[k], (((0,), (0,)), ((), ())), preferred_element_type=F32)
        ri = lax.div(lax.broadcasted_iota(jnp.int32, (256, 256), 0), GW)
        ci = lax.div(lax.broadcasted_iota(jnp.int32, (256, 256), 1), GW)
        keep = ri == ci
        for t in range(9):
            part = jnp.where(keep, m[:, (8 - t) * 256 : (9 - t) * 256], 0.0)
            part = jnp.sum(part.reshape(4, GW, 256), axis=0)
            if k == 0:
                dcf[l, t * GW : (t + 1) * GW, :] = part
            else:
                dcf[l, t * GW : (t + 1) * GW, :] += part

    def ax(l, k, m):
        me = 2 * xl + c
        src = me if m < 3 else jnp.bitwise_xor(me, 2)
        s = hidg.at[l, rsl(k), blk(src)]
        to = dev(xl_=1 - xl) if m == 2 else dev(c_=1 - c)
        return rc(s, s, ax_s.at[l, k, m - 1], ax_r.at[l, k, m - 1], to)

    def ax_in(l, k, m):
        s = hidg.at[l, rsl(k), blk(jnp.bitwise_xor(2 * xl + c, m))]
        return rc(s, s, ax_s.at[l, k, m - 1], ax_r.at[l, k, m - 1], dev(c_=1 - c))

    def ax_start(l, k):
        ax(l, k, 2).start()
        ax(l, k, 1).start()

    def ax_forward(l, k):
        ax_in(l, k, 2).wait_recv()
        ax(l, k, 3).start()

    def ax_wait(l, k):
        for m in (1, 3):
            ax_in(l, k, m).wait_recv()

    def yto(s):
        return lax.rem(y + 1 + 2 * s, 4)

    far = lax.rem(y + 2, 4)
    half = rows // 2

    def hsl(k, s):
        return pl.ds(pl.multiple_of(k * rows + s * half, half), half)

    def ay(l, k, s):
        r = gg.at[l, rsl(k), blk(y)]
        return rc(r, r, ay_s.at[l, k, s], ay_r.at[l, k, s], dev(y_=yto(s)))

    def ay_in(l, k, s):
        r = gg.at[l, rsl(k), blk(yto(1 - s))]
        return rc(r, r, ay_s.at[l, k, s], ay_r.at[l, k, s], dev(y_=yto(s)))

    def ayf(l, k, s):
        r = gg.at[l, hsl(k, s), blk(yto(1 - s))]
        return rc(r, r, ay_s.at[l, k, 2 + s], ay_r.at[l, k, 2 + s], dev(y_=yto(s)))

    def ayf_in(l, k, s):
        r = gg.at[l, hsl(k, s), blk(far)]
        return rc(r, r, ay_s.at[l, k, 2 + s], ay_r.at[l, k, 2 + s], dev(y_=yto(s)))

    def ay_start(l, k):
        for s in (0, 1):
            ay(l, k, s).start()

    def ay_forward(l, k):
        for s in (0, 1):
            ay_in(l, k, s).wait_recv()
            ayf(l, k, s).start()

    def ay_wait(l, k):
        for s in (0, 1):
            ayf_in(l, k, s).wait_recv()

    def ryf(l, k, s):
        return rc(
            rys.at[hsl(k, s), blk(far)], ryr.at[l, 2, hsl(k, s)],
            ry_s.at[l, k, 2 + s], ry_r.at[l, k, 2 + s], dev(y_=yto(s)),
        )

    def ry(l, k, s):
        return rc(
            rys.at[rsl(k), blk(yto(s))], ryr.at[l, s, rsl(k)],
            ry_s.at[l, k, s], ry_r.at[l, k, s], dev(y_=yto(s)),
        )

    def mix_far(l):
        @pl.loop(0, CH)
        def _(k):
            p = jnp.dot(hidg[l, rsl(k), :], wbuf[l, :, blk(far)], preferred_element_type=F32)
            rys[rsl(k), blk(far)] = p.astype(BF16)
            for s in (0, 1):
                ryf(l, k, s).start()

    def mix_near(l):
        @pl.loop(0, 2 * CH)
        def _(i):
            k, s = lax.div(i, 2), lax.rem(i, 2)
            tmp[...] = jnp.dot(hidg[l, rsl(k), :], wbuf[l, :, blk(yto(s))], preferred_element_type=F32)
            ryf(l, k, s).wait_recv()
            tmp[pl.ds(pl.multiple_of(s * half, half), half), :] += ryr[l, 2, hsl(k, s), :].astype(F32)
            rys[rsl(k), blk(yto(s))] = tmp[...].astype(BF16)
            ry(l, k, s).start()

    def mix_own(l):
        @pl.loop(0, CH)
        def _(k):
            p = jnp.dot(hidg[l, rsl(k), :], wbuf[l, :, blk(y)], preferred_element_type=F32)
            rys[rsl(k), blk(y)] = p.astype(BF16)

    def mixed(l, k):
        total = rys[rsl(k), blk(y)].astype(F32)
        for s in (0, 1):
            ry(l, k, s).wait_recv()
            total = total + ryr[l, s, rsl(k), :].astype(F32)
        return total

    def ry_drain(l):
        for k in range(CH):
            for s in (0, 1):
                ry(l, k, s).wait_send()
                ryf(l, k, s).wait_send()

    def rx(l, k, m):
        kb = jnp.bitwise_xor(2 * xl + c, m)
        return rc(
            rxs.at[rsl(k), blk(kb)], rxr.at[l, m - 1, rsl(k)],
            rx_s.at[l, k, m - 1], rx_r.at[l, k, m - 1],
            dev(xl_=1 - xl) if m == 2 else dev(c_=1 - c),
        )

    def back_block(l, k, m):
        kb = jnp.bitwise_xor(2 * xl + c, m)
        return kb, lax.dot_general(
            gg[l, rsl(k), :], wbuf[l, blk(kb), :], (((1,), (1,)), ((), ())), preferred_element_type=F32
        )

    def back_far(l):
        @pl.loop(0, CH)
        def _(k):
            kb, p = back_block(l, k, 3)
            rxs[rsl(k), blk(kb)] = p.astype(BF16)
            rx(l, k, 3).start()

    def back_near(l):
        @pl.loop(0, CH)
        def _(k):
            kb, p = back_block(l, k, 2)
            rx(l, k, 3).wait_recv()
            rxs[rsl(k), blk(kb)] = (p + rxr[l, 2, rsl(k), :].astype(F32)).astype(BF16)
            rx(l, k, 2).start()

    def back_own(l):
        @pl.loop(0, CH)
        def _(k):
            kb, p = back_block(l, k, 1)
            rxs[rsl(k), blk(kb)] = p.astype(BF16)
            rx(l, k, 1).start()
            kb, p = back_block(l, k, 0)
            rxs[rsl(k), blk(kb)] = p.astype(BF16)

    def mix_backward(l):
        back_far(l)
        back_near(l)
        back_own(l)

    def grad_hidden(l, k):
        total = rxs[rsl(k), blk(2 * xl + c)].astype(F32)
        for m in (1, 2):
            rx(l, k, m).wait_recv()
            total = total + rxr[l, m - 1, rsl(k), :].astype(F32)
        return total

    def rx_drain(l):
        for k in range(CH):
            for m in (1, 2, 3):
                rx(l, k, m).wait_send()

    def zrows(zs):
        return blk(lax.div(zs, 2), 512)

    def zcols(zs):
        return blk(lax.rem(zs, 2), 512)

    zfar = lax.rem(z + 2, 4)

    def zlanes(zs, h):
        return blk(2 * lax.rem(zs, 2) + jnp.where(h == 0, 1 - xh, xh))

    def daf(l, h, s):
        return rc(
            dws.at[l, blk(2 * lax.div(zfar, 2) + s), zlanes(zfar, h)], dar.at[l, 2, h, blk(s)],
            da_s.at[l, h, 2 + s], da_r.at[l, h, 2 + s], dev(z_=zto(s)),
        )

    def da(l, h, s):
        zo = zto(s)
        return rc(
            dws.at[l, zrows(zo), zlanes(zo, h)], dar.at[l, s, h],
            da_s.at[l, h, s], da_r.at[l, h, s], dev(z_=zo),
        )

    def weight_block(l, zo, h):
        return lax.dot_general(
            hidg[l, :, zrows(zo)], gg[l, :, zlanes(zo, h)], (((0,), (0,)), ((), ())), preferred_element_type=F32
        )

    def weight_far(l):
        @pl.loop(0, 2)
        def _(h):
            dws[l, zrows(zfar), zlanes(zfar, h)] = weight_block(l, zfar, h).astype(BF16)
            for s in (0, 1):
                daf(l, h, s).start()

    def weight_near(l):
        @pl.loop(0, 4)
        def _(i):
            h, s = lax.div(i, 2), lax.rem(i, 2)
            zo = zto(s)
            quad[...] = weight_block(l, zo, h)
            daf(l, h, s).wait_recv()
            hs = blk(s)
            quad[hs, :] += dar[l, 2, h, hs, :].astype(F32)
            dws[l, zrows(zo), zlanes(zo, h)] = quad[...].astype(BF16)
            da(l, h, s).start()

    def weight_own(l):
        @pl.loop(0, 2)
        def _(h):
            dws[l, zrows(z), zlanes(z, h)] = weight_block(l, z, h).astype(BF16)

    def db(l):
        return rc(dbs.at[l, 0], dbr.at[l], db_s.at[l], db_r.at[l], dev(xh_=1 - xh))

    def dw_sum(l, h):
        t = dws[l, zrows(z), zlanes(z, h)].astype(F32)
        for s in (0, 1):
            da(l, h, s).wait_recv()
            t = t + dar[l, s, h].astype(F32)
        dbs[l, h] = t.astype(BF16)
        if h == 0:
            db(l).start()

    def dc(l, h):
        src = dcs_.at[l, pl.ds(h * 256, 256)]
        dst = dcr_.at[l, c]
        self_ = jnp.logical_and(home, c == h)
        return (
            self_,
            lambda: pltpu.make_async_copy(src, dst, dc_r.at[l, c]),
            lambda: rc(src, dst, dc_s.at[l, h], dc_r.at[l, c], dev(z_=zt, xl_=xt, c_=h)),
        )

    def dw_b(l):
        db(l).wait_recv()
        t = (dbs[l, 1].astype(F32) + dbr[l].astype(F32)) * scale
        dcs_[l] = t.astype(BF16)
        for h in (0, 1):
            self_, loc, rem = dc(l, h)

            @pl.when(self_)
            def _():
                loc().start()

            @pl.when(jnp.logical_not(self_))
            def _():
                rem().start()

    def dw_c(l):
        for cc in (0, 1):
            part = dcr_.at[l, cc]
            rc(part, part, dc_s.at[l, 0], dc_r.at[l, cc], dev(c_=1 - c)).wait_recv()
            gmix[l, :, cc * 256 : (cc + 1) * 256] = dcr_[l, cc].astype(F32)

    def dw_drain(l):
        for h in (0, 1):
            for s in (0, 1):
                da(l, h, s).wait_send()
                daf(l, h, s).wait_send()
        db(l).wait_send()
        for h in (0, 1):
            self_, _, rem = dc(l, h)

            @pl.when(jnp.logical_not(self_))
            def _():
                rem().wait_send()

    def de(l, o):
        dt = lax.rem(d + o, 8)
        return rc(dcc.at[l, dt], dcv.at[l, o], de_s.at[l, o], de_r.at[l, o], dpdev(o))

    def conv_grad_send(l):
        for i in range(8):
            dcc[l, i] = dcf[l, i * 72 : (i + 1) * 72, :].astype(BF16)
        for o in range(1, 8):
            de(l, o).start()

    def conv_grad_done(l):
        for o in range(1, 8):
            de(l, o).wait_recv()
        t = dcc[l, d].astype(F32)
        for o in range(1, 8):
            t = t + dcv[l, o].astype(F32)
        gconv[l] = t * scale

    for o in range(1, 8):
        cv(0, o).start()
    w1_start(0)
    gg[1, :, blk(y)] = cot[...]
    for k in range(CH):
        ay_start(1, k)
    for b in range(3):
        pad[b, :, 0] = jnp.zeros((nimg, 8, 256), F32)
        pad[b, :, 9] = jnp.zeros((nimg, 8, 256), F32)
    conv_weights(0)
    w2_start(0)
    conv_forward(0, 0, img[rsl(0), :].astype(F32))
    ax_start(0, 0)
    w3_start(0)
    w1_start(1)
    w_forward(0, 0)
    conv_forward(0, 1, img[rsl(1), :].astype(F32))
    ax_start(0, 1)
    ay_forward(1, 0)
    ax_forward(0, 0)
    w_forward(0, 1)
    w2_start(1)
    for o in range(1, 8):
        cv(1, o).start()
    ay_forward(1, 1)
    ax_forward(0, 1)
    for k in range(CH):
        ax_wait(0, k)
    w_wait(0)
    mix_far(0)
    w3_start(1)
    w_forward(1, 0)
    mix_near(0)
    w_forward(1, 1)
    mix_own(0)
    conv_weights(1)
    for k in range(CH):
        ay_wait(1, k)
    w_wait(1)
    mix_backward(1)
    for k in range(CH):
        xf = (img[rsl(k), :].astype(F32) + mixed(0, k)).astype(BF16)
        x1[rsl(k), :] = xf
        conv_forward(1, k, xf.astype(F32))
        ax_start(1, k)
        gp = (grad_hidden(1, k) * slope[1, rsl(k), :]).astype(BF16)
        field = conv_backward(1, k, gp.astype(F32))
        gg[0, rsl(k), blk(y)] = (cot[rsl(k), :].astype(F32) + field).astype(BF16)
        ay_start(0, k)
    for k in range(CH):
        ax_forward(1, k)
    ay_forward(0, 0)
    ry_drain(0)
    rx_drain(1)
    for k in range(CH):
        ax_wait(1, k)
    weight_far(1)
    ay_forward(0, 1)
    weight_near(1)
    mix_far(1)
    weight_own(1)
    for k in range(CH):
        ay_wait(0, k)
    back_far(0)
    weight_far(0)
    back_near(0)
    back_own(0)
    dw_sum(1, 0)
    weight_near(0)
    dw_sum(1, 1)
    weight_own(0)
    for k in range(CH):
        conv_weight_grad(1, k, x1[rsl(k), :])
    conv_grad_send(1)
    dw_b(1)
    mix_near(1)
    dw_sum(0, 0)
    gp = (grad_hidden(0, 0) * slope[0, rsl(0), :]).astype(BF16)
    field = conv_backward(0, 0, gp.astype(F32))
    gimg[rsl(0), :] = (gg[0, rsl(0), blk(y)].astype(F32) + field).astype(BF16)
    dw_sum(0, 1)
    gp = (grad_hidden(0, 1) * slope[0, rsl(1), :]).astype(BF16)
    field = conv_backward(0, 1, gp.astype(F32))
    gimg[rsl(1), :] = (gg[0, rsl(1), blk(y)].astype(F32) + field).astype(BF16)
    dw_b(0)
    mix_own(1)
    for k in range(CH):
        conv_weight_grad(0, k, img[rsl(k), :])
    conv_grad_send(0)
    for k in range(CH):
        feat[rsl(k), :] = (x1[rsl(k), :].astype(F32) + mixed(1, k)).astype(BF16)
    conv_grad_done(1)
    dw_c(1)
    dw_c(0)
    conv_grad_done(0)
    ry_drain(1)
    rx_drain(0)
    for l in range(2):
        w_drain(l)
        dw_drain(l)
        for o in range(1, 8):
            cv(l, o).wait_send()
            de(l, o).wait_send()
        for k in range(CH):
            for m in (1, 2, 3):
                ax(l, k, m).wait_send()
            for s in (0, 1):
                ay(l, k, s).wait_send()
                ayf(l, k, s).wait_send()


def per_device(images, cotangent, conv_weight, mix_weight):
    n, s, _, w = images.shape
    nrow = n * s * s
    rows = nrow // CH
    scale = 1.0 / math.sqrt(nrow * lax.axis_size("dp"))
    vm = pl.BlockSpec(memory_space=pltpu.VMEM)
    dma = pltpu.SemaphoreType.DMA
    scratch = [
        pltpu.VMEM((2, 1024, 1024), BF16),
        pltpu.VMEM((2, nrow, 1024), BF16),
        pltpu.VMEM((2, nrow, 1024), BF16),
        pltpu.VMEM((2, nrow, 256), F32),
        pltpu.VMEM((CH, rows, 2304), BF16),
        pltpu.VMEM((3, rows // 64, 10, 8, 256), F32),
        pltpu.VMEM((2, 2304, 256), BF16),
        pltpu.VMEM((2, 2304, 256), BF16),
        pltpu.VMEM((2, 8, 72, 256), BF16),
        pltpu.VMEM((576, 256), F32),
        pltpu.VMEM((nrow, 256), BF16),
        pltpu.VMEM((nrow, 1024), BF16),
        pltpu.VMEM((2, 3, nrow, 256), BF16),
        pltpu.VMEM((nrow, 1024), BF16),
        pltpu.VMEM((2, 3, nrow, 256), BF16),
        pltpu.VMEM((rows, 256), F32),
        pltpu.VMEM((512, 256), F32),
        pltpu.VMEM((2, 1024, 1024), BF16),
        pltpu.VMEM((2, 3, 2, 512, 256), BF16),
        pltpu.VMEM((2, 2, 512, 256), BF16),
        pltpu.VMEM((2, 512, 256), BF16),
        pltpu.VMEM((2, 512, 256), BF16),
        pltpu.VMEM((2, 2, 256, 256), BF16),
        pltpu.VMEM((2, 576, 256), F32),
        pltpu.VMEM((2, 8, 72, 256), BF16),
        pltpu.VMEM((2, 8, 72, 256), BF16),
        dma((2, 8)), dma((2, 8)),
        dma((2, 2)), dma((2, 2)),
        dma((2,)), dma((2,)),
        dma((2, 2, 4)), dma((2, 2, 4)),
        dma((2, CH, 3)), dma((2, CH, 3)),
        dma((2, CH, 4)), dma((2, CH, 4)),
        dma((2, CH, 4)), dma((2, CH, 4)),
        dma((2, CH, 3)), dma((2, CH, 3)),
        dma((2, 2, 4)), dma((2, 2, 4)),
        dma((2,)), dma((2,)),
        dma((2, 2)), dma((2, 2)),
        dma((2, 8)), dma((2, 8)),
    ]
    feat, gimg, gconv, gmix = pl.pallas_call(
        functools.partial(kernel, scale),
        name="resblocks",
        out_shape=(
            jax.ShapeDtypeStruct((nrow, w), BF16),
            jax.ShapeDtypeStruct((nrow, w), BF16),
            jax.ShapeDtypeStruct(conv_weight.shape, F32),
            jax.ShapeDtypeStruct(mix_weight.shape, F32),
        ),
        in_specs=[vm] * 4,
        out_specs=[vm] * 4,
        scratch_shapes=scratch,
        compiler_params=pltpu.CompilerParams(
            collective_id=0, has_side_effects=True, vmem_limit_bytes=62 << 20
        ),
    )(images.reshape(nrow, w), cotangent.reshape(nrow, w), conv_weight, mix_weight)
    return feat.reshape(images.shape), gimg.reshape(images.shape), gconv, gmix


def solution(mesh):
    specs = (
        P("dp", None, None, "group"),
        P("dp", None, None, "group"),
        P(None, "dp", "group"),
        P(None, "group", "dp"),
    )
    return jax.shard_map(per_device, mesh=mesh, in_specs=specs, out_specs=specs, check_vma=False)
```
